32 devices in a mesh: gz: 4 (over y, x), phi: 8 (over z, core).
Axes of the slice: x: 2, y: 2, z: 4, core: 2. Of those that a mesh axis runs over, the one named last changes fastest.
Arguments:
- potential_in: float32 [256, 512, 256], P('phi', 'gz'), may hold values from -6 to 6
- charge: float32 [256, 512, 256], P('phi', 'gz'), may hold values from -6 to 6
- cell_kind: int32 [256, 512, 256], P('phi', 'gz'), may hold values from 0 to 2, as said below
Outputs:
- potential: float32 [256, 512, 256], P('phi', 'gz')
- shift_r: float32 [256, 512, 256], P('phi', 'gz')
- shift_rphi: float32 [256, 512, 256], P('phi', 'gz')
The draws below stay inside these ranges and needn't reach their ends.
Inputs may be any that keep to these rules, and one draw needn't show every extreme that they name: `cell_kind`: 0 marks a free cell, 1 an electrode cell held at zero potential, 2 a boundary cell held at its given potential.
All inputs are finite; a program needn't handle non-finite values.
Results may differ from the reference program's by a relative error of at most 0.000073.
Values sent between devices are 32-bit elements; how exact they have to be, the bound alone decides.
A program may use at most 128 MiB of HBM per device.

```python
import math
import jax
import jax.numpy as jnp

NR = 256
PASSES = 3
NPHI = 256
NZ = 512


def draw_cell_kind(key, part):
    values = jax.random.randint(jax.random.fold_in(key, 17), (NPHI, NZ, NR), 0, 16)
    return jnp.where(values == 0, 1, jnp.where(values == 1, 2, 0)).astype(jnp.int32)


def levels(own_key, shape, split, least, top_value):
    factor_of = 1.0
    for position, blocks in split:
        draws = jax.random.uniform(jax.random.fold_in(jax.random.fold_in(own_key, 6), position), (blocks,), jnp.float32, least / len(split), top_value / len(split))
        factor_of = factor_of * jnp.repeat(jnp.exp(draws), shape[position] // blocks).reshape((-1,) + (1,) * (len(shape) - 1 - position))
    return factor_of


def gaussian(key, extent, deviation, bound, split=(), held_as=jnp.bfloat16):
    level = levels(key, extent, split, -0.22, 0.18) if split else 1.0
    result = jax.random.normal(key, extent, jnp.float32) * deviation * level
    return jnp.minimum(jnp.maximum(result, -bound), bound).astype(held_as)


def setup_inputs(seed: int = 0) -> dict:
    splits = jax.random.split(jax.random.key(seed), 4)
    return {
        "potential_in": gaussian(splits[0], (NPHI, NZ, NR), 1.0, 6.0, ((0, 8), (1, 4)), jnp.float32),
        "charge": gaussian(splits[1], (NPHI, NZ, NR), 1.0, 6.0, ((0, 8), (1, 4)), jnp.float32),
        "cell_kind": draw_cell_kind(jax.random.fold_in(splits[3], 71), 0),
    }


relax_weight = 1.5


def coefficients(radial, sectors):
    radius = radial * 0.5 + jnp.arange(radial, dtype=jnp.float32) + 0.5
    step_phi = 2.0 * math.pi / sectors
    outward = 1.0 + 0.5 / radius
    inward = 1.0 - 0.5 / radius
    beside_all = 1.0 / (radius * step_phi) ** 2
    diag = 4.0 + 2.0 * beside_all
    return radius, step_phi, outward, inward, beside_all, diag


def radial_next(field):
    return jnp.concatenate([field[:, :, 1:], jnp.zeros_like(field[:, :, :1])], 2)


def radial_prev(field):
    return jnp.concatenate([jnp.zeros_like(field[:, :, :1]), field[:, :, :-1]], 2)


def reference(potential_in, charge, cell_kind):
    sectors, depth, radial = potential_in.shape
    radius, step_phi, outward, inward, beside_all, diag = coefficients(radial, sectors)
    parity = (jnp.arange(sectors, dtype=jnp.int32)[:, None, None] + jnp.arange(depth, dtype=jnp.int32)[None, :, None] + jnp.arange(radial, dtype=jnp.int32)[None, None, :]) % 2
    free = cell_kind == 0
    field = jnp.where(cell_kind == 1, jnp.zeros_like(potential_in), potential_in)
    for sweep in range(PASSES):
        for color in (0, 1):
            next_z = jnp.concatenate([field[:, 1:], jnp.zeros_like(field[:, :1])], 1)
            prev_z = jnp.concatenate([jnp.zeros_like(field[:, :1]), field[:, :-1]], 1)
            total = outward * radial_next(field) + inward * radial_prev(field) + beside_all * (jnp.roll(field, -1, 0) + jnp.roll(field, 1, 0)) + next_z + prev_z
            target = (total + charge) / diag
            update = jnp.logical_and(parity == color, free)
            field = jnp.where(update, field + relax_weight * (target - field), field)
    field_r = -0.5 * (radial_next(field) - radial_prev(field))
    field_phi = -0.5 * (jnp.roll(field, -1, 0) - jnp.roll(field, 1, 0)) / (radius * step_phi)
    drift_r = (field_r + 0.3 * field_phi) / (1.09 * 32.0)
    drift_phi = (field_phi - 0.3 * field_r) / (1.09 * 32.0)
    shift_r = jnp.flip(jnp.cumsum(jnp.flip(drift_r, 1), 1), 1)
    shift_rphi = jnp.flip(jnp.cumsum(jnp.flip(drift_phi, 1), 1), 1)
    return field, shift_r, shift_rphi
```

```python
import functools
import math

import jax
import jax.numpy as jnp
import numpy as np
from jax import lax
from jax.experimental import pallas as pl
from jax.experimental.pallas import tpu as pltpu
from jax.sharding import PartitionSpec as P

PASSES = 3
RELAX = 1.5
FIXED = 1e30
MESH = pl.DeviceIdType.MESH
PAD = 16
LANES = 128
RED, BLACK = 0, 1


def parity_mask():
    row = lax.broadcasted_iota(jnp.int32, (8, LANES), 0)
    lane = lax.broadcasted_iota(jnp.int32, (8, LANES), 1)
    return (row + lane) % 2 == 0


def beside(halves, lane):
    ahead = [pltpu.roll(x, LANES - 1, axis=1) for x in halves]
    behind = [pltpu.roll(x, 1, axis=1) for x in halves]
    last = len(halves) - 1
    outer = [ahead[h] if h == last else jnp.where(lane == LANES - 1, ahead[h + 1], ahead[h]) for h in range(last + 1)]
    inner = [behind[h] if h == 0 else jnp.where(lane == 0, behind[h - 1], behind[h]) for h in range(last + 1)]
    return outer, inner


def relax_kernel(
    slabs, rings, pot, chg, kind, coef, full, carry,
    pot_in, chg_in, kind_in, red, black, source, zsend, zrecv, crecv, total, total_recv, edge, edge_recv,
    load_sem, jsend_sem, jrecv_sem, zsend_sem, zrecv_sem, csend_sem, crecv_sem,
    fsend_sem, frecv_sem, tsend_sem, trecv_sem, esend_sem, erecv_sem,
):
    halves = red.shape[0]
    sectors, depth, radial = pot_in.shape
    pairs = sectors // 2
    tiles = depth // 8
    slab = lax.axis_index("gz")
    ring = lax.axis_index("phi")
    right, left = lax.rem(ring + 1, rings), lax.rem(ring + rings - 1, rings)
    has_next, has_prev = slab < slabs - 1, slab > 0
    whole_rows = pl.ds(PAD, depth)
    halo = (pairs, pairs + 1)

    def loads(slot, planes, rows):
        return [
            pltpu.make_async_copy(src.at[planes, rows], dst.at[planes, rows], load_sem.at[slot, n])
            for n, (src, dst) in enumerate(((pot, pot_in), (chg, chg_in), (kind, kind_in)))
        ]

    every, middle = pl.ds(0, sectors), pl.ds(8, depth - 16)
    ends = [loads(pairs, every, pl.ds(0, 8)), loads(pairs + 1, every, pl.ds(depth - 8, 8))]

    def pair_loads(p):
        return loads(p, pl.ds(2 * p, 2), middle)

    for batch in ends:
        for copy in batch:
            copy.start()
    for p in (0, pairs - 1):
        for copy in pair_loads(p):
            copy.start()

    def start_pair(p, _):
        for copy in pair_loads(p):
            copy.start()
        return 0

    lax.fori_loop(1, pairs - 1, start_pair, 0)

    barrier = pltpu.get_barrier_semaphore()
    for neighbour in (left, right):
        pl.semaphore_signal(barrier, inc=1, device_id={"phi": neighbour}, device_id_type=MESH)
    for step in range(1, slabs):
        peer = lax.rem(slab + step, slabs)
        for column in (left, ring, right):
            pl.semaphore_signal(barrier, inc=1, device_id={"gz": peer, "phi": column}, device_id_type=MESH)

    nothing = jnp.zeros((8, LANES), jnp.float32)
    held = jnp.full((8, LANES), FIXED, jnp.float32)
    for h in range(halves):
        for rows in (pl.ds(PAD - 8, 8), pl.ds(PAD + depth, 8)):
            for p in range(black.shape[1]):
                black[h, p, rows, :] = nothing
            for p in range(pairs):
                red[h, p, rows, :] = nothing
                source[RED, h, p, rows, :] = held

    def prepare(p, which):
        mask = parity_mask()
        for tile in which:
            rows, out = pl.ds(8 * tile, 8), pl.ds(PAD + 8 * tile, 8)
            for h in range(halves):
                lanes = pl.ds(LANES * h, LANES)
                plane, charges = [], []
                for side in range(2):
                    what = kind_in[2 * p + side, rows, lanes]
                    plane.append(jnp.where(what == 1, 0.0, pot_in[2 * p + side, rows, lanes]))
                    charges.append(jnp.where(what == 0, chg_in[2 * p + side, rows, lanes], FIXED))
                red[h, p, out, :] = jnp.where(mask, plane[0], plane[1])
                black[h, p, out, :] = jnp.where(mask, plane[1], plane[0])
                source[RED, h, p, out, :] = jnp.where(mask, charges[0], charges[1])
                source[BLACK, h, p, out, :] = jnp.where(mask, charges[1], charges[0])

    def fresh_tile(color, p, near, before, after, tile):
        own, other = (red, black) if color == RED else (black, red)
        mask = parity_mask()
        lane = lax.broadcasted_iota(jnp.int32, (8, LANES), 1)
        first, second = (before, after) if color == RED else (after, before)
        at = PAD + 8 * tile
        rows = pl.ds(at, 8)
        here = [other[h, near, rows, :] for h in range(halves)]
        outer, inner = beside(here, lane)
        result = []
        for h in range(halves):
            around = here[h] + jnp.where(mask, other[h, first, rows, :], other[h, second, rows, :])
            along = other[h, near, pl.ds(at - 1, 8), :] + other[h, near, pl.ds(at + 1, 8), :]
            put = source[color, h, p, rows, :]
            old = own[h, p, rows, :]
            gathered = (put + along) + (coef[0, h] * outer[h] + coef[1, h] * inner[h]) + coef[2, h] * around
            fresh = coef[3, h] * gathered - (RELAX - 1.0) * old
            result.append((jnp.where(put < 0.5 * FIXED, fresh, old), here[h]))
        return result

    def update(color, p, near, before, after, which):
        own = red if color == RED else black
        for tile in which:
            for h, (value, _) in enumerate(fresh_tile(color, p, near, before, after, tile)):
                own[h, p, pl.ds(PAD + 8 * tile, 8), :] = value

    def halo_black(exchange):
        return pairs + 2 * exchange, pairs + 2 * exchange + 1

    def jcopies(exchange, side):
        edge_pair = (pairs - 1, 0)[side]
        moves = [(black, (slice(None), edge_pair), (slice(None), halo_black(exchange)[side]))]
        if exchange == 0:
            moves.append((red, (slice(None), edge_pair), (slice(None), halo[side])))
            moves.append((source, (RED, slice(None), edge_pair), (RED, slice(None), halo[side])))
        return [
            pltpu.make_async_remote_copy(
                src_ref=ref.at[(*src, whole_rows)],
                dst_ref=ref.at[(*dst, whole_rows)],
                send_sem=jsend_sem.at[exchange, n, side],
                recv_sem=jrecv_sem.at[exchange, n, side],
                device_id={"phi": (right, left)[side]},
                device_id_type=MESH,
            )
            for n, (ref, src, dst) in enumerate(moves)
        ]

    slots = (lambda exchange: (0, PASSES) if exchange == 0 else (exchange,))

    def zcopy(slot, side):
        return pltpu.make_async_remote_copy(
            src_ref=zsend.at[slot, side],
            dst_ref=zrecv.at[slot, side],
            send_sem=zsend_sem.at[slot, side],
            recv_sem=zrecv_sem.at[slot, side],
            device_id={"gz": (lax.rem(slab + 1, slabs), lax.rem(slab + slabs - 1, slabs))[side]},
            device_id_type=MESH,
        )

    def ccopy(exchange, side, face):
        return pltpu.make_async_remote_copy(
            src_ref=zsend.at[exchange, side, :, (pairs - 1, 0)[face]],
            dst_ref=crecv.at[exchange, side, face],
            send_sem=csend_sem.at[exchange, side, face],
            recv_sem=crecv_sem.at[exchange, side, face],
            device_id={
                "gz": (lax.rem(slab + 1, slabs), lax.rem(slab + slabs - 1, slabs))[side],
                "phi": (right, left)[face],
            },
            device_id_type=MESH,
        )

    def zmoves(exchange, side):
        return [zcopy(slot, side) for slot in slots(exchange)] + [ccopy(exchange, side, face) for face in range(2)]

    def when_sides(exchange, gate, act):
        for side in range(2):
            @pl.when(gate[side])
            def _():
                for copy in zmoves(exchange, side):
                    act(copy)

    def send_z(exchange):
        for h in range(halves):
            for p in range(pairs):
                zsend[exchange, 0, h, p] = black[h, p, pl.ds(PAD + depth - 2, 2), :]
                zsend[exchange, 1, h, p] = black[h, p, pl.ds(PAD, 2), :]
                if exchange == 0:
                    for side, at in ((0, PAD + depth - 1), (1, PAD)):
                        zsend[PASSES, side, h, p, pl.ds(0, 1), :] = red[h, p, pl.ds(at, 1), :]
                        zsend[PASSES, side, h, p, pl.ds(1, 1), :] = source[RED, h, p, pl.ds(at, 1), :]

    def start_z(exchange):
        when_sides(exchange, (has_next, has_prev), lambda copy: copy.start())

    def take_z(exchange):
        for side in range(2):
            @pl.when((has_prev, has_next)[side])
            def _():
                for copy in zmoves(exchange, side):
                    copy.wait_recv()
                two = pl.ds((PAD - 2, PAD + depth)[side], 2)
                one = pl.ds((PAD - 1, PAD + depth)[side], 1)
                for h in range(halves):
                    for p in range(pairs):
                        black[h, p, two, :] = zrecv[exchange, side, h, p]
                        if exchange == 0:
                            red[h, p, one, :] = zrecv[PASSES, side, h, p, pl.ds(0, 1), :]
                            source[RED, h, p, one, :] = zrecv[PASSES, side, h, p, pl.ds(1, 1), :]
                    for face in range(2):
                        black[h, halo_black(exchange)[face], two, :] = crecv[exchange, side, face, h]

    def start_j(exchange):
        for side in range(2):
            for copy in jcopies(exchange, side):
                copy.start()

    def loop(low, high, body):
        lax.fori_loop(low, high, lambda p, _: (body(p), 0)[1], 0)

    inside = range(1, tiles - 1)
    whole = range(tiles)
    rims = (0, tiles - 1)

    def red_inside(p):
        update(RED, p, p, p - 1, p + 1, inside)

    def red_edges(exchange):
        low, high = halo_black(exchange)
        take_z(exchange)
        loop(1, pairs - 1, lambda p: update(RED, p, p, p - 1, p + 1, (-1, 0, tiles - 1, tiles)))
        for side in range(2):
            for copy in jcopies(exchange, side):
                copy.wait_recv()
            if exchange == 0:
                for copy in jcopies(exchange, 1 - side):
                    copy.wait_send()
        for side in range(2):
            p, before, after = ((0, low, 1), (pairs - 1, pairs - 2, high))[side]
            update(RED, p, p, before, after, range(-1, tiles + 1))
            p, near, before, after = ((halo[0], low, low, 0), (halo[1], high, pairs - 1, high))[side]
            update(RED, p, near, before, after, whole)

    for batch in ends:
        for copy in batch:
            copy.wait()
    loop(0, pairs, lambda p: prepare(p, rims))
    send_z(0)
    pl.semaphore_wait(barrier, 2 + 3 * (slabs - 1))
    start_z(0)
    for p in (0, pairs - 1):
        for copy in pair_loads(p):
            copy.wait()
        prepare(p, inside)
    start_j(0)

    def arrive(p):
        for copy in pair_loads(p):
            copy.wait()
        prepare(p, inside)

    arrive(1)

    def arrive_and_update(p):
        arrive(p)
        red_inside(p - 1)

    loop(2, pairs - 1, arrive_and_update)
    red_inside(pairs - 2)

    for sweep in range(PASSES):
        if sweep > 0:
            loop(1, pairs - 1, red_inside)
        red_edges(sweep)
        if sweep > 0:
            for side in range(2):
                for copy in jcopies(sweep, side):
                    copy.wait_send()
        if sweep < PASSES - 1:
            update(BLACK, 0, 0, halo[0], 1, whole)
            update(BLACK, pairs - 1, pairs - 1, pairs - 2, halo[1], whole)
            start_j(sweep + 1)
            loop(1, pairs - 1, lambda p: update(BLACK, p, p, p - 1, p + 1, rims))
            send_z(sweep + 1)
            start_z(sweep + 1)
            loop(1, pairs - 1, lambda p: update(BLACK, p, p, p - 1, p + 1, inside))

    def finish(p, before, after):
        mask = parity_mask()
        sums = [[jnp.zeros((8, LANES), jnp.float32) for _ in range(2)] for _ in range(halves)]
        for tile in whole:
            rows = pl.ds(8 * tile, 8)
            for h, (value, near) in enumerate(fresh_tile(BLACK, p, p, before, after, tile)):
                for side in range(2):
                    plane = jnp.where(mask, near, value) if side == 0 else jnp.where(mask, value, near)
                    full[2 * p + 1 + side, rows, pl.ds(LANES * h, LANES)] = plane
                    sums[h][side] = sums[h][side] + plane
        for h in range(halves):
            for side in range(2):
                total[h, pl.ds(2 * p + side, 1), :] = jnp.sum(sums[h][side], axis=0, keepdims=True)

    def fcopy(side):
        return pltpu.make_async_remote_copy(
            src_ref=full.at[(sectors, 1)[side]],
            dst_ref=full.at[(0, sectors + 1)[side]],
            send_sem=fsend_sem.at[side],
            recv_sem=frecv_sem.at[side],
            device_id={"phi": (right, left)[side]},
            device_id_type=MESH,
        )

    finish(0, halo[0], 1)
    finish(pairs - 1, pairs - 2, halo[1])
    for side in range(2):
        fcopy(side).start()
    loop(1, pairs - 1, lambda p: finish(p, p - 1, p + 1))
    for h in range(halves):
        edge[0, h] = total[h, pl.ds(sectors - 1, 1), :]
        edge[1, h] = total[h, pl.ds(0, 1), :]

    def tcopies(step):
        lower = lax.rem(slab + slabs - step, slabs)
        return [
            pltpu.make_async_remote_copy(
                src_ref=total,
                dst_ref=total_recv.at[step - 1],
                send_sem=tsend_sem.at[step - 1],
                recv_sem=trecv_sem.at[step - 1],
                device_id={"gz": lower},
                device_id_type=MESH,
            )
        ] + [
            pltpu.make_async_remote_copy(
                src_ref=edge.at[face],
                dst_ref=edge_recv.at[step - 1, face],
                send_sem=esend_sem.at[step - 1, face],
                recv_sem=erecv_sem.at[step - 1, face],
                device_id={"gz": lower, "phi": (right, left)[face]},
                device_id_type=MESH,
            )
            for face in range(2)
        ]

    for step in range(1, slabs):
        @pl.when(slab >= step)
        def _():
            for copy in tcopies(step):
                copy.start()

    carry[...] = jnp.zeros(carry.shape, jnp.float32)
    for step in range(1, slabs):
        @pl.when(slab + step < slabs)
        def _():
            for copy in tcopies(step):
                copy.wait_recv()
            for h in range(halves):
                carry[h, pl.ds(1, sectors), :] = carry[h, pl.ds(1, sectors), :] + total_recv[step - 1, h]
                for face, at in ((0, 0), (1, sectors + 1)):
                    carry[h, pl.ds(at, 1), :] = carry[h, pl.ds(at, 1), :] + edge_recv[step - 1, face, h]

    for side in range(2):
        fcopy(side).wait_recv()
        fcopy(side).wait_send()
    for step in range(1, slabs):
        @pl.when(slab >= step)
        def _():
            for copy in tcopies(step):
                copy.wait_send()
    for sweep in range(PASSES):
        when_sides(sweep, (has_next, has_prev), lambda copy: copy.wait_send())


def drift_kernel(
    coef, full, carry, potential, shift_r, shift_phi,
    runs, ones, twos, sums, out_r, out_phi, pot_sem, out_sem,
):
    halves, tall = runs.shape[0], runs.shape[1]
    sectors = full.shape[0] - 2
    depth = full.shape[1]
    pairs = sectors // 2
    tiles = depth // 8
    row = lax.broadcasted_iota(jnp.int32, (8, LANES), 0)
    lane = lax.broadcasted_iota(jnp.int32, (8, LANES), 1)

    parts = pot_sem.shape[0]

    def pot_copy(part):
        count = sectors // parts
        return pltpu.make_async_copy(
            full.at[pl.ds(1 + part * count, count)], potential.at[pl.ds(part * count, count)], pot_sem.at[part]
        )

    def out_copies(pair, slot):
        planes = pl.ds(2 * pair, 2)
        return [
            pltpu.make_async_copy(out_r.at[slot], shift_r.at[planes], out_sem.at[slot, 0]),
            pltpu.make_async_copy(out_phi.at[slot], shift_phi.at[planes], out_sem.at[slot, 1]),
        ]

    for part in range(parts):
        pot_copy(part).start()

    def integrate(plane, slot):
        for h in range(halves):
            after = jnp.broadcast_to(carry[h, pl.ds(plane, 1), :], (8, LANES))
            run = jnp.where(row == 0, after, 0.0)
            for ref in (runs, ones, twos):
                ref[h, pl.ds(depth, 8), :] = run
            for tile in range(tiles - 1, -1, -1):
                run = run + full[plane, pl.ds(8 * tile, 8), pl.ds(LANES * h, LANES)]
                runs[h, pl.ds(8 * tile, 8), :] = run
        for h in range(halves):
            for src, dst, hop in ((runs, ones, 1), (ones, twos, 2)):
                for tile in range(tiles - 1, -1, -1):
                    at = 8 * tile
                    dst[h, pl.ds(at, 8), :] = src[h, pl.ds(at, 8), :] + src[h, pl.ds(at + hop, 8), :]
            for tile in range(tiles - 1, -1, -1):
                at = 8 * tile
                sums[slot, h, pl.ds(at, 8), :] = twos[h, pl.ds(at, 8), :] + twos[h, pl.ds(at + 4, 8), :]

    def combine(low, here, high, out, side):
        for tile in range(tiles):
            rows = pl.ds(8 * tile, 8)
            outer, inner = beside([sums[here, h, rows, :] for h in range(halves)], lane)
            for h in range(halves):
                lanes = pl.ds(LANES * h, LANES)
                along_r = coef[0, h] * outer[h] + coef[1, h] * inner[h]
                across = sums[high, h, rows, :] - sums[low, h, rows, :]
                out_r[out, side, rows, lanes] = along_r + coef[3, h] * across
                out_phi[out, side, rows, lanes] = coef[2, h] * across - 0.3 * along_r

    integrate(0, 0)
    integrate(1, 1)

    def body(g, _):
        now = lax.rem(g, 2)
        new, old = 2 * now, 2 - 2 * now
        integrate(2 * g, new)
        integrate(2 * g + 1, new + 1)

        @pl.when(g >= 3)
        def _():
            for copy in out_copies(g - 3, now):
                copy.wait()

        combine(old, old + 1, new, now, 0)
        combine(old + 1, new, new + 1, now, 1)
        for copy in out_copies(g - 1, now):
            copy.start()
        return 0

    lax.fori_loop(1, pairs + 1, body, 0)
    for g in (pairs - 1, pairs):
        for copy in out_copies(g - 1, g % 2):
            copy.wait()
    for part in range(parts):
        pot_copy(part).wait()


def coefficients(radial, sectors):
    radius = radial * 0.5 + np.arange(radial, dtype=np.float64) + 0.5
    step_phi = 2.0 * math.pi / sectors
    around = 1.0 / (radius * step_phi) ** 2
    diag = 4.0 + 2.0 * around
    has_next = np.arange(radial) < radial - 1
    has_prev = np.arange(radial) > 0
    drift = 1.0 / (1.09 * 32.0)
    across = -0.5 * drift / (radius * step_phi)
    relax = [(1.0 + 0.5 / radius) * has_next, (1.0 - 0.5 / radius) * has_prev, around, RELAX / diag]
    shift = [-0.5 * drift * has_next, 0.5 * drift * has_prev, across, 0.3 * across]

    def tiled(rows):
        halves = np.stack(rows).astype(np.float32).reshape(len(rows), radial // LANES, 1, LANES)
        return jnp.asarray(np.ascontiguousarray(np.broadcast_to(halves, halves.shape[:2] + (8, LANES))))

    return tiled(relax), tiled(shift)


def local(slabs, rings, potential_in, charge, cell_kind):
    sectors, depth, radial = potential_in.shape
    pairs, halves = sectors // 2, radial // LANES
    tall = depth + 2 * PAD
    relax, shift = coefficients(radial, sectors * rings)
    any_spec = pl.BlockSpec(memory_space=pl.ANY)
    vmem_spec = pl.BlockSpec(memory_space=pltpu.VMEM)
    f32 = jnp.float32
    dma = pltpu.SemaphoreType.DMA
    full, carry = pl.pallas_call(
        functools.partial(relax_kernel, slabs, rings),
        out_shape=(
            pltpu.VMEM((sectors + 2, depth, radial), f32),
            pltpu.VMEM((halves, sectors + 2, LANES), f32),
        ),
        in_specs=[any_spec, any_spec, any_spec, vmem_spec],
        out_specs=(vmem_spec, vmem_spec),
        scratch_shapes=[
            pltpu.VMEM((sectors, depth, radial), f32),
            pltpu.VMEM((sectors, depth, radial), f32),
            pltpu.VMEM((sectors, depth, radial), jnp.int32),
            pltpu.VMEM((halves, pairs + 2, tall, LANES), f32),
            pltpu.VMEM((halves, pairs + 2 * PASSES, tall, LANES), f32),
            pltpu.VMEM((2, halves, pairs + 2, tall, LANES), f32),
            pltpu.VMEM((PASSES + 1, 2, halves, pairs, 2, LANES), f32),
            pltpu.VMEM((PASSES + 1, 2, halves, pairs, 2, LANES), f32),
            pltpu.VMEM((PASSES, 2, 2, halves, 2, LANES), f32),
            pltpu.VMEM((halves, sectors, LANES), f32),
            pltpu.VMEM((slabs - 1, halves, sectors, LANES), f32),
            pltpu.VMEM((2, halves, 1, LANES), f32),
            pltpu.VMEM((slabs - 1, 2, halves, 1, LANES), f32),
            dma((pairs + 2, 3)),
            dma((PASSES, 3, 2)),
            dma((PASSES, 3, 2)),
            dma((PASSES + 1, 2)),
            dma((PASSES + 1, 2)),
            dma((PASSES, 2, 2)),
            dma((PASSES, 2, 2)),
            dma((2,)),
            dma((2,)),
            dma((slabs - 1,)),
            dma((slabs - 1,)),
            dma((slabs - 1, 2)),
            dma((slabs - 1, 2)),
        ],
        compiler_params=pltpu.CompilerParams(
            collective_id=0, has_side_effects=True, vmem_limit_bytes=48 * 2**20
        ),
    )(potential_in, charge, cell_kind, relax)

    full = pltpu.with_memory_space_constraint(full, pltpu.VMEM)
    carry = pltpu.with_memory_space_constraint(carry, pltpu.VMEM)
    block = jax.ShapeDtypeStruct((sectors, depth, radial), f32)
    return pl.pallas_call(
        drift_kernel,
        out_shape=(block, block, block),
        in_specs=[vmem_spec, vmem_spec, vmem_spec],
        out_specs=(any_spec,) * 3,
        scratch_shapes=[
            pltpu.VMEM((halves, depth + 8, LANES), f32),
            pltpu.VMEM((halves, depth + 8, LANES), f32),
            pltpu.VMEM((halves, depth + 8, LANES), f32),
            pltpu.VMEM((4, halves, depth, LANES), f32),
            pltpu.VMEM((2, 2, depth, radial), f32),
            pltpu.VMEM((2, 2, depth, radial), f32),
            dma((4,)),
            dma((2, 2)),
        ],
        compiler_params=pltpu.CompilerParams(vmem_limit_bytes=16 * 2**20),
    )(shift, full, carry)


def solution(mesh):
    spec = P("phi", "gz", None)
    body = functools.partial(local, mesh.shape["gz"], mesh.shape["phi"])
    return jax.shard_map(body, mesh=mesh, in_specs=(spec,) * 3, out_specs=(spec,) * 3, check_vma=False)
```

```python
import functools
import math

import jax
import jax.numpy as jnp
from jax import lax
from jax.experimental import pallas as pl
from jax.experimental.pallas import tpu as pltpu
from jax.sharding import PartitionSpec as P

PASSES = 3
RELAX = 1.5
FIXED = 1e30
MESH = pl.DeviceIdType.MESH
PAD = 16
LANES = 128
RED, BLACK = 0, 1
UNROLL = 2


def parity_mask():
    row = lax.broadcasted_iota(jnp.int32, (8, LANES), 0)
    lane = lax.broadcasted_iota(jnp.int32, (8, LANES), 1)
    return (row + lane) % 2 == 0


def beside(halves, lane):
    ahead = [pltpu.roll(x, LANES - 1, axis=1) for x in halves]
    behind = [pltpu.roll(x, 1, axis=1) for x in halves]
    last = len(halves) - 1
    outer = [ahead[h] if h == last else jnp.where(lane == LANES - 1, ahead[h + 1], ahead[h]) for h in range(last + 1)]
    inner = [behind[h] if h == 0 else jnp.where(lane == 0, behind[h - 1], behind[h]) for h in range(last + 1)]
    return outer, inner


def geometry(half, radial, sectors):
    cell = lax.broadcasted_iota(jnp.int32, (8, LANES), 1) + LANES * half
    radius = radial * 0.5 + cell.astype(jnp.float32) + 0.5
    step = radius * (2.0 * math.pi / sectors)
    around = 1.0 / (step * step)
    outward = jnp.where(cell < radial - 1, 1.0 + 0.5 / radius, 0.0)
    inward = jnp.where(cell > 0, 1.0 - 0.5 / radius, 0.0)
    return outward, inward, around, 4.0 + 2.0 * around, step


def relax_kernel(
    slabs, rings, pot, chg, kind, full, carry,
    coef, pot_in, chg_in, kind_in, red, black, source, zsend, zrecv, crecv, total, total_recv, edge, edge_recv,
    load_sem, jsend_sem, jrecv_sem, zsend_sem, zrecv_sem, csend_sem, crecv_sem,
    fsend_sem, frecv_sem, tsend_sem, trecv_sem, esend_sem, erecv_sem,
):
    halves = red.shape[0]
    sectors, depth, radial = pot_in.shape
    pairs = sectors // 2
    tiles = depth // 8
    slab = lax.axis_index("gz")
    ring = lax.axis_index("phi")
    right, left = lax.rem(ring + 1, rings), lax.rem(ring + rings - 1, rings)
    has_next, has_prev = slab < slabs - 1, slab > 0
    whole_rows = pl.ds(PAD, depth)
    halo = (pairs, pairs + 1)

    def loads(slot, planes, rows):
        return [
            pltpu.make_async_copy(src.at[planes, rows], dst.at[planes, rows], load_sem.at[slot, n])
            for n, (src, dst) in enumerate(((pot, pot_in), (chg, chg_in), (kind, kind_in)))
        ]

    every, middle = pl.ds(0, sectors), pl.ds(8, depth - 16)
    ends = [loads(pairs, every, pl.ds(0, 8)), loads(pairs + 1, every, pl.ds(depth - 8, 8))]

    def pair_loads(p):
        return loads(p, pl.ds(2 * p, 2), middle)

    for batch in ends:
        for copy in batch:
            copy.start()
    for p in (0, pairs - 1):
        for copy in pair_loads(p):
            copy.start()

    def start_pair(p, _):
        for copy in pair_loads(p):
            copy.start()
        return 0

    lax.fori_loop(1, pairs - 1, start_pair, 0)

    barrier = pltpu.get_barrier_semaphore()
    for neighbour in (left, right):
        pl.semaphore_signal(barrier, inc=1, device_id={"phi": neighbour}, device_id_type=MESH)
    for step in range(1, slabs):
        peer = lax.rem(slab + step, slabs)
        for column in (left, ring, right):
            pl.semaphore_signal(barrier, inc=1, device_id={"gz": peer, "phi": column}, device_id_type=MESH)

    for h in range(halves):
        outward, inward, around_i, diag, _ = geometry(h, radial, sectors * rings)
        for n, values in enumerate((outward, inward, around_i, RELAX / diag)):
            coef[n, h] = values

    nothing = jnp.zeros((8, LANES), jnp.float32)
    held = jnp.full((8, LANES), FIXED, jnp.float32)
    for h in range(halves):
        for rows in (pl.ds(PAD - 8, 8), pl.ds(PAD + depth, 8)):
            for p in range(black.shape[1]):
                black[h, p, rows, :] = nothing
            for p in range(pairs):
                red[h, p, rows, :] = nothing
                source[RED, h, p, rows, :] = held

    def prepare(p, which):
        mask = parity_mask()
        for tile in which:
            rows, out = pl.ds(8 * tile, 8), pl.ds(PAD + 8 * tile, 8)
            for h in range(halves):
                lanes = pl.ds(LANES * h, LANES)
                plane, charges = [], []
                for side in range(2):
                    what = kind_in[2 * p + side, rows, lanes]
                    plane.append(jnp.where(what == 1, 0.0, pot_in[2 * p + side, rows, lanes]))
                    charges.append(jnp.where(what == 0, chg_in[2 * p + side, rows, lanes], FIXED))
                red[h, p, out, :] = jnp.where(mask, plane[0], plane[1])
                black[h, p, out, :] = jnp.where(mask, plane[1], plane[0])
                source[RED, h, p, out, :] = jnp.where(mask, charges[0], charges[1])
                source[BLACK, h, p, out, :] = jnp.where(mask, charges[1], charges[0])

    def fresh_tile(color, p, near, before, after, tile):
        own, other = (red, black) if color == RED else (black, red)
        mask = parity_mask()
        lane = lax.broadcasted_iota(jnp.int32, (8, LANES), 1)
        first, second = (before, after) if color == RED else (after, before)
        at = PAD + 8 * tile
        rows = pl.ds(at, 8)
        here = [other[h, near, rows, :] for h in range(halves)]
        outer, inner = beside(here, lane)
        result = []
        for h in range(halves):
            around = here[h] + jnp.where(mask, other[h, first, rows, :], other[h, second, rows, :])
            along = other[h, near, pl.ds(at - 1, 8), :] + other[h, near, pl.ds(at + 1, 8), :]
            put = source[color, h, p, rows, :]
            old = own[h, p, rows, :]
            gathered = (put + along) + (coef[0, h] * outer[h] + coef[1, h] * inner[h]) + coef[2, h] * around
            fresh = coef[3, h] * gathered - (RELAX - 1.0) * old
            result.append((jnp.where(put < 0.5 * FIXED, fresh, old), here[h]))
        return result

    def update(color, p, near, before, after, which):
        own = red if color == RED else black
        for tile in which:
            for h, (value, _) in enumerate(fresh_tile(color, p, near, before, after, tile)):
                own[h, p, pl.ds(PAD + 8 * tile, 8), :] = value

    def halo_black(exchange):
        return pairs + 2 * exchange, pairs + 2 * exchange + 1

    def jcopies(exchange, side):
        edge_pair = (pairs - 1, 0)[side]
        moves = [(black, (slice(None), edge_pair), (slice(None), halo_black(exchange)[side]))]
        if exchange == 0:
            moves.append((red, (slice(None), edge_pair), (slice(None), halo[side])))
            moves.append((source, (RED, slice(None), edge_pair), (RED, slice(None), halo[side])))
        return [
            pltpu.make_async_remote_copy(
                src_ref=ref.at[(*src, whole_rows)],
                dst_ref=ref.at[(*dst, whole_rows)],
                send_sem=jsend_sem.at[exchange, n, side],
                recv_sem=jrecv_sem.at[exchange, n, side],
                device_id={"phi": (right, left)[side]},
                device_id_type=MESH,
            )
            for n, (ref, src, dst) in enumerate(moves)
        ]

    slots = (lambda exchange: (0, PASSES) if exchange == 0 else (exchange,))

    def zcopy(slot, side):
        return pltpu.make_async_remote_copy(
            src_ref=zsend.at[slot, side],
            dst_ref=zrecv.at[slot, side],
            send_sem=zsend_sem.at[slot, side],
            recv_sem=zrecv_sem.at[slot, side],
            device_id={"gz": (lax.rem(slab + 1, slabs), lax.rem(slab + slabs - 1, slabs))[side]},
            device_id_type=MESH,
        )

    def ccopy(exchange, side, face):
        return pltpu.make_async_remote_copy(
            src_ref=zsend.at[exchange, side, :, (pairs - 1, 0)[face]],
            dst_ref=crecv.at[exchange, side, face],
            send_sem=csend_sem.at[exchange, side, face],
            recv_sem=crecv_sem.at[exchange, side, face],
            device_id={
                "gz": (lax.rem(slab + 1, slabs), lax.rem(slab + slabs - 1, slabs))[side],
                "phi": (right, left)[face],
            },
            device_id_type=MESH,
        )

    def zmoves(exchange, side):
        return [zcopy(slot, side) for slot in slots(exchange)] + [ccopy(exchange, side, face) for face in range(2)]

    def when_sides(exchange, gate, act):
        for side in range(2):
            @pl.when(gate[side])
            def _():
                for copy in zmoves(exchange, side):
                    act(copy)

    def send_z(exchange):
        for h in range(halves):
            for p in range(pairs):
                zsend[exchange, 0, h, p] = black[h, p, pl.ds(PAD + depth - 2, 2), :]
                zsend[exchange, 1, h, p] = black[h, p, pl.ds(PAD, 2), :]
                if exchange == 0:
                    for side, at in ((0, PAD + depth - 1), (1, PAD)):
                        zsend[PASSES, side, h, p, pl.ds(0, 1), :] = red[h, p, pl.ds(at, 1), :]
                        zsend[PASSES, side, h, p, pl.ds(1, 1), :] = source[RED, h, p, pl.ds(at, 1), :]

    def start_z(exchange):
        when_sides(exchange, (has_next, has_prev), lambda copy: copy.start())

    def take_z(exchange):
        for side in range(2):
            @pl.when((has_prev, has_next)[side])
            def _():
                for copy in zmoves(exchange, side):
                    copy.wait_recv()
                two = pl.ds((PAD - 2, PAD + depth)[side], 2)
                one = pl.ds((PAD - 1, PAD + depth)[side], 1)
                for h in range(halves):
                    for p in range(pairs):
                        black[h, p, two, :] = zrecv[exchange, side, h, p]
                        if exchange == 0:
                            red[h, p, one, :] = zrecv[PASSES, side, h, p, pl.ds(0, 1), :]
                            source[RED, h, p, one, :] = zrecv[PASSES, side, h, p, pl.ds(1, 1), :]
                    for face in range(2):
                        black[h, halo_black(exchange)[face], two, :] = crecv[exchange, side, face, h]

    def start_j(exchange):
        for side in range(2):
            for copy in jcopies(exchange, side):
                copy.start()

    def loop(low, high, body, unroll=UNROLL):
        odd = (high - low) % unroll

        def several(n, _):
            for step in range(unroll):
                body(low + odd + n * unroll + step)
            return 0

        for p in range(low, low + odd):
            body(p)
        lax.fori_loop(0, (high - low) // unroll, several, 0)

    inside = range(1, tiles - 1)
    whole = range(tiles)
    rims = (0, tiles - 1)

    def red_inside(p):
        update(RED, p, p, p - 1, p + 1, inside)

    def red_edges(exchange):
        low, high = halo_black(exchange)
        take_z(exchange)
        loop(1, pairs - 1, lambda p: update(RED, p, p, p - 1, p + 1, (-1, 0, tiles - 1, tiles)))
        for side in range(2):
            for copy in jcopies(exchange, side):
                copy.wait_recv()
            if exchange == 0:
                for copy in jcopies(exchange, 1 - side):
                    copy.wait_send()
        for side in range(2):
            p, before, after = ((0, low, 1), (pairs - 1, pairs - 2, high))[side]
            update(RED, p, p, before, after, range(-1, tiles + 1))
            p, near, before, after = ((halo[0], low, low, 0), (halo[1], high, pairs - 1, high))[side]
            update(RED, p, near, before, after, whole)

    for batch in ends:
        for copy in batch:
            copy.wait()
    loop(0, pairs, lambda p: prepare(p, rims))
    send_z(0)
    pl.semaphore_wait(barrier, 2 + 3 * (slabs - 1))
    start_z(0)
    for p in (0, pairs - 1):
        for copy in pair_loads(p):
            copy.wait()
        prepare(p, inside)
    start_j(0)

    def arrive(p):
        for copy in pair_loads(p):
            copy.wait()
        prepare(p, inside)

    arrive(1)

    def arrive_and_update(p):
        arrive(p)
        red_inside(p - 1)

    loop(2, pairs - 1, arrive_and_update, 1)
    red_inside(pairs - 2)

    for sweep in range(PASSES):
        if sweep > 0:
            loop(1, pairs - 1, red_inside)
        red_edges(sweep)
        if sweep > 0:
            for side in range(2):
                for copy in jcopies(sweep, side):
                    copy.wait_send()
        if sweep < PASSES - 1:
            update(BLACK, 0, 0, halo[0], 1, whole)
            update(BLACK, pairs - 1, pairs - 1, pairs - 2, halo[1], whole)
            start_j(sweep + 1)
            loop(1, pairs - 1, lambda p: update(BLACK, p, p, p - 1, p + 1, rims))
            send_z(sweep + 1)
            start_z(sweep + 1)
            loop(1, pairs - 1, lambda p: update(BLACK, p, p, p - 1, p + 1, inside))

    def finish(p, before, after):
        mask = parity_mask()
        sums = [[jnp.zeros((8, LANES), jnp.float32) for _ in range(2)] for _ in range(halves)]
        for tile in whole:
            rows = pl.ds(8 * tile, 8)
            for h, (value, near) in enumerate(fresh_tile(BLACK, p, p, before, after, tile)):
                for side in range(2):
                    plane = jnp.where(mask, near, value) if side == 0 else jnp.where(mask, value, near)
                    full[2 * p + 1 + side, rows, pl.ds(LANES * h, LANES)] = plane
                    sums[h][side] = sums[h][side] + plane
        for h in range(halves):
            for side in range(2):
                total[h, pl.ds(2 * p + side, 1), :] = jnp.sum(sums[h][side], axis=0, keepdims=True)

    def fcopy(side):
        return pltpu.make_async_remote_copy(
            src_ref=full.at[(sectors, 1)[side]],
            dst_ref=full.at[(0, sectors + 1)[side]],
            send_sem=fsend_sem.at[side],
            recv_sem=frecv_sem.at[side],
            device_id={"phi": (right, left)[side]},
            device_id_type=MESH,
        )

    finish(0, halo[0], 1)
    finish(pairs - 1, pairs - 2, halo[1])
    for side in range(2):
        fcopy(side).start()
    loop(1, pairs - 1, lambda p: finish(p, p - 1, p + 1))
    for h in range(halves):
        edge[0, h] = total[h, pl.ds(sectors - 1, 1), :]
        edge[1, h] = total[h, pl.ds(0, 1), :]

    def tcopies(step):
        lower = lax.rem(slab + slabs - step, slabs)
        return [
            pltpu.make_async_remote_copy(
                src_ref=total,
                dst_ref=total_recv.at[step - 1],
                send_sem=tsend_sem.at[step - 1],
                recv_sem=trecv_sem.at[step - 1],
                device_id={"gz": lower},
                device_id_type=MESH,
            )
        ] + [
            pltpu.make_async_remote_copy(
                src_ref=edge.at[face],
                dst_ref=edge_recv.at[step - 1, face],
                send_sem=esend_sem.at[step - 1, face],
                recv_sem=erecv_sem.at[step - 1, face],
                device_id={"gz": lower, "phi": (right, left)[face]},
                device_id_type=MESH,
            )
            for face in range(2)
        ]

    for step in range(1, slabs):
        @pl.when(slab >= step)
        def _():
            for copy in tcopies(step):
                copy.start()

    carry[...] = jnp.zeros(carry.shape, jnp.float32)
    for step in range(1, slabs):
        @pl.when(slab + step < slabs)
        def _():
            for copy in tcopies(step):
                copy.wait_recv()
            for h in range(halves):
                carry[h, pl.ds(1, sectors), :] = carry[h, pl.ds(1, sectors), :] + total_recv[step - 1, h]
                for face, at in ((0, 0), (1, sectors + 1)):
                    carry[h, pl.ds(at, 1), :] = carry[h, pl.ds(at, 1), :] + edge_recv[step - 1, face, h]

    for side in range(2):
        fcopy(side).wait_recv()
        fcopy(side).wait_send()
    for step in range(1, slabs):
        @pl.when(slab >= step)
        def _():
            for copy in tcopies(step):
                copy.wait_send()
    for sweep in range(PASSES):
        when_sides(sweep, (has_next, has_prev), lambda copy: copy.wait_send())


def drift_kernel(
    rings, full, carry, potential, shift_r, shift_phi,
    coef, runs, ones, twos, sums, out_r, out_phi, pot_sem, out_sem,
):
    halves = runs.shape[1]
    sectors = full.shape[0] - 2
    depth = full.shape[1]
    pairs = sectors // 2
    tiles = depth // 8
    row = lax.broadcasted_iota(jnp.int32, (8, LANES), 0)
    lane = lax.broadcasted_iota(jnp.int32, (8, LANES), 1)

    pot_copy = pltpu.make_async_copy(full.at[pl.ds(1, sectors)], potential, pot_sem)
    pot_copy.start()
    drift = 1.0 / (1.09 * 32.0)
    for h in range(halves):
        outward, inward, _, _, step = geometry(h, LANES * halves, sectors * rings)
        coef[0, h] = jnp.where(outward > 0.0, -0.5 * drift, 0.0)
        coef[1, h] = jnp.where(inward > 0.0, 0.5 * drift, 0.0)
        coef[2, h] = -0.5 * drift / step
        coef[3, h] = 0.3 * (-0.5 * drift / step)

    def out_copies(pair):
        planes = pl.ds(2 * pair, 2)
        return [
            pltpu.make_async_copy(src.at[planes], dst.at[planes], out_sem.at[n, pair])
            for n, (src, dst) in enumerate(((out_r, shift_r), (out_phi, shift_phi)))
        ]

    def integrate(plane, slot):
        for h in range(halves):
            after = jnp.broadcast_to(carry[h, pl.ds(plane, 1), :], (8, LANES))
            run = jnp.where(row == 0, after, 0.0)
            for ref in (runs, ones, twos):
                ref[slot, h, pl.ds(depth, 8), :] = run
            for tile in range(tiles - 1, -1, -1):
                run = run + full[plane, pl.ds(8 * tile, 8), pl.ds(LANES * h, LANES)]
                runs[slot, h, pl.ds(8 * tile, 8), :] = run
        for h in range(halves):
            for src, dst, hop in ((runs, ones, 1), (ones, twos, 2)):
                for tile in range(tiles - 1, -1, -1):
                    at = 8 * tile
                    dst[slot, h, pl.ds(at, 8), :] = src[slot, h, pl.ds(at, 8), :] + src[slot, h, pl.ds(at + hop, 8), :]
            for tile in range(tiles - 1, -1, -1):
                at = 8 * tile
                sums[plane, h, pl.ds(at, 8), :] = twos[slot, h, pl.ds(at, 8), :] + twos[slot, h, pl.ds(at + 4, 8), :]

    def combine(plane):
        for tile in range(tiles):
            rows = pl.ds(8 * tile, 8)
            outer, inner = beside([sums[plane, h, rows, :] for h in range(halves)], lane)
            for h in range(halves):
                lanes = pl.ds(LANES * h, LANES)
                along_r = coef[0, h] * outer[h] + coef[1, h] * inner[h]
                across = sums[plane + 1, h, rows, :] - sums[plane - 1, h, rows, :]
                out_r[plane - 1, rows, lanes] = along_r + coef[3, h] * across
                out_phi[plane - 1, rows, lanes] = coef[2, h] * across - 0.3 * along_r

    def emit(pair):
        combine(2 * pair + 1)
        combine(2 * pair + 2)
        for copy in out_copies(pair):
            copy.start()

    for plane in range(4):
        integrate(plane, plane % 2)

    def body(g, _):
        integrate(2 * g, 0)
        integrate(2 * g + 1, 1)
        emit(g - 2)
        return 0

    lax.fori_loop(2, pairs + 1, body, 0)
    emit(pairs - 1)

    def drain(pair, _):
        for copy in out_copies(pair):
            copy.wait()
        return 0

    lax.fori_loop(0, pairs, drain, 0)
    pot_copy.wait()


def local(slabs, rings, potential_in, charge, cell_kind):
    sectors, depth, radial = potential_in.shape
    pairs, halves = sectors // 2, radial // LANES
    tall = depth + 2 * PAD
    any_spec = pl.BlockSpec(memory_space=pl.ANY)
    vmem_spec = pl.BlockSpec(memory_space=pltpu.VMEM)
    f32 = jnp.float32
    dma = pltpu.SemaphoreType.DMA
    full, carry = pl.pallas_call(
        functools.partial(relax_kernel, slabs, rings),
        out_shape=(
            pltpu.VMEM((sectors + 2, depth, radial), f32),
            pltpu.VMEM((halves, sectors + 2, LANES), f32),
        ),
        in_specs=[any_spec] * 3,
        out_specs=(vmem_spec, vmem_spec),
        scratch_shapes=[
            pltpu.VMEM((4, halves, 8, LANES), f32),
            pltpu.VMEM((sectors, depth, radial), f32),
            pltpu.VMEM((sectors, depth, radial), f32),
            pltpu.VMEM((sectors, depth, radial), jnp.int32),
            pltpu.VMEM((halves, pairs + 2, tall, LANES), f32),
            pltpu.VMEM((halves, pairs + 2 * PASSES, tall, LANES), f32),
            pltpu.VMEM((2, halves, pairs + 2, tall, LANES), f32),
            pltpu.VMEM((PASSES + 1, 2, halves, pairs, 2, LANES), f32),
            pltpu.VMEM((PASSES + 1, 2, halves, pairs, 2, LANES), f32),
            pltpu.VMEM((PASSES, 2, 2, halves, 2, LANES), f32),
            pltpu.VMEM((halves, sectors, LANES), f32),
            pltpu.VMEM((slabs - 1, halves, sectors, LANES), f32),
            pltpu.VMEM((2, halves, 1, LANES), f32),
            pltpu.VMEM((slabs - 1, 2, halves, 1, LANES), f32),
            dma((pairs + 2, 3)),
            dma((PASSES, 3, 2)),
            dma((PASSES, 3, 2)),
            dma((PASSES + 1, 2)),
            dma((PASSES + 1, 2)),
            dma((PASSES, 2, 2)),
            dma((PASSES, 2, 2)),
            dma((2,)),
            dma((2,)),
            dma((slabs - 1,)),
            dma((slabs - 1,)),
            dma((slabs - 1, 2)),
            dma((slabs - 1, 2)),
        ],
        compiler_params=pltpu.CompilerParams(
            collective_id=0, has_side_effects=True, vmem_limit_bytes=48 * 2**20
        ),
    )(potential_in, charge, cell_kind)

    full = pltpu.with_memory_space_constraint(full, pltpu.VMEM)
    carry = pltpu.with_memory_space_constraint(carry, pltpu.VMEM)
    block = jax.ShapeDtypeStruct((sectors, depth, radial), f32)
    return pl.pallas_call(
        functools.partial(drift_kernel, rings),
        out_shape=(block, block, block),
        in_specs=[vmem_spec, vmem_spec],
        out_specs=(any_spec,) * 3,
        scratch_shapes=[
            pltpu.VMEM((4, halves, 8, LANES), f32),
            pltpu.VMEM((2, halves, depth + 8, LANES), f32),
            pltpu.VMEM((2, halves, depth + 8, LANES), f32),
            pltpu.VMEM((2, halves, depth + 8, LANES), f32),
            pltpu.VMEM((sectors + 2, halves, depth, LANES), f32),
            pltpu.VMEM((sectors, depth, radial), f32),
            pltpu.VMEM((sectors, depth, radial), f32),
            dma,
            dma((2, pairs)),
        ],
        compiler_params=pltpu.CompilerParams(vmem_limit_bytes=24 * 2**20),
    )(full, carry)


def solution(mesh):
    spec = P("phi", "gz", None)
    body = functools.partial(local, mesh.shape["gz"], mesh.shape["phi"])
    return jax.shard_map(body, mesh=mesh, in_specs=(spec,) * 3, out_specs=(spec,) * 3, check_vma=False)
```

```python
import functools
import math

import jax
import jax.numpy as jnp
from jax import lax
from jax.experimental import pallas as pl
from jax.experimental.pallas import tpu as pltpu
from jax.sharding import PartitionSpec as P

PASSES = 3
RELAX = 1.5
FIXED = 1e30
MESH = pl.DeviceIdType.MESH
PAD = 16
LANES = 128
RED, BLACK = 0, 1
UNROLL = 2


def parity_mask():
    row = lax.broadcasted_iota(jnp.int32, (8, LANES), 0)
    lane = lax.broadcasted_iota(jnp.int32, (8, LANES), 1)
    return ((row + lane) & 1) == 0


def beside(halves, lane):
    ahead = [pltpu.roll(x, LANES - 1, axis=1) for x in halves]
    behind = [pltpu.roll(x, 1, axis=1) for x in halves]
    last = len(halves) - 1
    outer = [ahead[h] if h == last else lax.select(lane == LANES - 1, ahead[h + 1], ahead[h]) for h in range(last + 1)]
    inner = [behind[h] if h == 0 else lax.select(lane == 0, behind[h - 1], behind[h]) for h in range(last + 1)]
    return outer, inner


def geometry(half, radial, sectors):
    cell = lax.broadcasted_iota(jnp.int32, (8, LANES), 1) + LANES * half
    radius = radial * 0.5 + cell.astype(jnp.float32) + 0.5
    step = radius * (2.0 * math.pi / sectors)
    around = 1.0 / (step * step)
    outward = jnp.where(cell < radial - 1, 1.0 + 0.5 / radius, 0.0)
    inward = jnp.where(cell > 0, 1.0 - 0.5 / radius, 0.0)
    return outward, inward, around, 4.0 + 2.0 * around, step


def relax_kernel(
    slabs, rings, pot, chg, kind, full, carry,
    coef, pot_in, chg_in, kind_in, red, black, source, mixed, zsend, zrecv, crecv,
    partial, total, total_recv, edge, edge_recv,
    load_sem, jsend_sem, jrecv_sem, zsend_sem, zrecv_sem, csend_sem, crecv_sem,
    tsend_sem, trecv_sem, esend_sem, erecv_sem,
):
    halves = red.shape[0]
    sectors, depth, radial = pot_in.shape
    pairs = sectors // 2
    tiles = depth // 8
    slab = lax.axis_index("gz")
    ring = lax.axis_index("phi")
    right, left = lax.rem(ring + 1, rings), lax.rem(ring + rings - 1, rings)
    has_next, has_prev = slab < slabs - 1, slab > 0
    halo = (pairs, pairs + 1)

    def loads(slot, planes, rows):
        return [
            pltpu.make_async_copy(src.at[planes, rows], dst.at[planes, rows], load_sem.at[slot, n])
            for n, (src, dst) in enumerate(((pot, pot_in), (chg, chg_in), (kind, kind_in)))
        ]

    every, middle = pl.ds(0, sectors), pl.ds(8, depth - 16)
    ends = [loads(pairs, every, pl.ds(0, 8)), loads(pairs + 1, every, pl.ds(depth - 8, 8))]

    def pair_loads(p):
        return loads(p, pl.ds(2 * p, 2), middle)

    for batch in ends:
        for copy in batch:
            copy.start()
    for p in (0, pairs - 1):
        for copy in pair_loads(p):
            copy.start()

    def start_pair(p, _):
        for copy in pair_loads(p):
            copy.start()
        return 0

    lax.fori_loop(1, pairs - 1, start_pair, 0)

    barrier = pltpu.get_barrier_semaphore()
    for neighbour in (left, right):
        pl.semaphore_signal(barrier, inc=1, device_id={"phi": neighbour}, device_id_type=MESH)
    for step in range(1, slabs):
        peer = lax.rem(slab + step, slabs)
        for column in (left, ring, right):
            pl.semaphore_signal(barrier, inc=1, device_id={"gz": peer, "phi": column}, device_id_type=MESH)

    for h in range(halves):
        outward, inward, around_i, diag, _ = geometry(h, radial, sectors * rings)
        for n, values in enumerate((outward, inward, around_i, RELAX / diag)):
            coef[n, h] = values

    nothing = jnp.zeros((8, LANES), jnp.float32)
    held = jnp.full((8, LANES), FIXED, jnp.float32)

    def clear(p, _):
        for h in range(halves):
            for rows in (pl.ds(PAD - 8, 8), pl.ds(PAD + depth, 8)):
                black[h, p, rows, :] = nothing
        return 0

    def clear_own(p, _):
        for h in range(halves):
            for rows in (pl.ds(PAD - 8, 8), pl.ds(PAD + depth, 8)):
                red[h, p, rows, :] = nothing
                source[RED, h, p, rows, :] = held
        return 0

    lax.fori_loop(0, black.shape[1], clear, 0)
    lax.fori_loop(0, pairs, clear_own, 0)

    def prepare(p, which):
        mask = parity_mask()
        for tile in which:
            rows, out = pl.ds(8 * tile, 8), pl.ds(PAD + 8 * tile, 8)
            for h in range(halves):
                lanes = pl.ds(LANES * h, LANES)
                plane, charges = [], []
                for side in range(2):
                    what = kind_in[2 * p + side, rows, lanes]
                    plane.append(lax.select(what == 1, nothing, pot_in[2 * p + side, rows, lanes]))
                    charges.append(lax.select(what == 0, chg_in[2 * p + side, rows, lanes], held))
                red[h, p, out, :] = lax.select(mask, plane[0], plane[1])
                black[h, p, out, :] = lax.select(mask, plane[1], plane[0])
                source[RED, h, p, out, :] = lax.select(mask, charges[0], charges[1])
                source[BLACK, h, p, out, :] = lax.select(mask, charges[1], charges[0])

    def fresh_tiles(color, p, near, before, after, which):
        own, other = (red, black) if color == RED else (black, red)
        mask = parity_mask()
        lane = lax.broadcasted_iota(jnp.int32, (8, LANES), 1)
        first, second = (before, after) if color == RED else (after, before)
        factor = [[coef[n, h] for n in range(4)] for h in range(halves)]
        for tile in which:
            at = PAD + 8 * tile
            rows = pl.ds(at, 8)
            here = [other[h, near, rows, :] for h in range(halves)]
            outer, inner = beside(here, lane)
            result = []
            for h in range(halves):
                out_c, in_c, around_c, scale = factor[h]
                around = here[h] + lax.select(mask, other[h, first, rows, :], other[h, second, rows, :])
                along = other[h, near, pl.ds(at - 1, 8), :] + other[h, near, pl.ds(at + 1, 8), :]
                put = source[color, h, p, rows, :]
                old = own[h, p, rows, :]
                gathered = (put + along) + (out_c * outer[h] + in_c * inner[h]) + around_c * around
                fresh = scale * gathered - (RELAX - 1.0) * old
                result.append((lax.select(put < 0.5 * FIXED, fresh, old), here[h]))
            yield tile, result

    def update(color, p, near, before, after, which):
        own = red if color == RED else black
        for tile, result in fresh_tiles(color, p, near, before, after, which):
            for h, (value, _) in enumerate(result):
                own[h, p, pl.ds(PAD + 8 * tile, 8), :] = value

    def halo_black(exchange):
        return pairs + 2 * exchange, pairs + 2 * exchange + 1

    def first_tiles(exchange):
        return tiles // 2 + 1 - exchange

    def piece_tiles(exchange, piece):
        cut = first_tiles(exchange)
        return (0, cut) if piece == 0 else (cut, tiles)

    def jcopies(exchange, side, piece):
        low, high = piece_tiles(exchange, piece)
        if exchange == PASSES:
            rows = pl.ds(8 * low, 8 * (high - low))
            moves = [(full.at[(sectors, 1)[side], rows], full.at[(0, sectors + 1)[side], rows])]
        else:
            rows = pl.ds(PAD + 8 * low, 8 * (high - low))
            edge_pair = (pairs - 1, 0)[side]
            moves = [(black.at[:, edge_pair, rows], black.at[:, halo_black(exchange)[side], rows])]
        if exchange == 0:
            moves.append((mixed.at[side, :, pl.ds(8 * low, 8 * (high - low))], red.at[:, halo[side], rows]))
        return [
            pltpu.make_async_remote_copy(
                src_ref=src,
                dst_ref=dst,
                send_sem=jsend_sem.at[exchange, n, side, piece],
                recv_sem=jrecv_sem.at[exchange, n, side, piece],
                device_id={"phi": (right, left)[side]},
                device_id_type=MESH,
            )
            for n, (src, dst) in enumerate(moves)
        ]

    def on_j(exchange, piece, act):
        for side in range(2):
            for copy in jcopies(exchange, side, piece):
                act(copy)

    def mix(side):
        p = (pairs - 1, 0)[side]
        mask = parity_mask()
        for tile in range(tiles):
            rows = pl.ds(PAD + 8 * tile, 8)
            for h in range(halves):
                values, charges = red[h, p, rows, :], pltpu.roll(source[RED, h, p, rows, :], 1, axis=1)
                both = (charges, values) if side == 0 else (values, charges)
                mixed[side, h, pl.ds(8 * tile, 8), :] = lax.select(mask, *both)

    def unmix(piece):
        for tile in range(*piece_tiles(0, piece)):
            rows = pl.ds(PAD + 8 * tile, 8)
            for side in range(2):
                for h in range(halves):
                    source[RED, h, halo[side], rows, :] = pltpu.roll(red[h, halo[side], rows, :], LANES - 1, axis=1)

    def zcopy(slot, side):
        return pltpu.make_async_remote_copy(
            src_ref=zsend.at[slot, side],
            dst_ref=zrecv.at[slot, side],
            send_sem=zsend_sem.at[slot, side],
            recv_sem=zrecv_sem.at[slot, side],
            device_id={"gz": (lax.rem(slab + 1, slabs), lax.rem(slab + slabs - 1, slabs))[side]},
            device_id_type=MESH,
        )

    def ccopy(exchange, side, face):
        return pltpu.make_async_remote_copy(
            src_ref=zsend.at[exchange, side, :, (pairs - 1, 0)[face]],
            dst_ref=crecv.at[exchange, side, face],
            send_sem=csend_sem.at[exchange, side, face],
            recv_sem=crecv_sem.at[exchange, side, face],
            device_id={
                "gz": (lax.rem(slab + 1, slabs), lax.rem(slab + slabs - 1, slabs))[side],
                "phi": (right, left)[face],
            },
            device_id_type=MESH,
        )

    def zmoves(exchange, side):
        rows = [zcopy(exchange, side)] + ([zcopy(PASSES, side)] if exchange == 0 else [])
        return [ccopy(exchange, side, face) for face in range(2)] + rows

    def on_z(exchange, act):
        for side in range(2):
            @pl.when((has_next, has_prev)[side])
            def _():
                for copy in zmoves(exchange, side):
                    act(copy)

    def send_z(exchange):
        def gather(p, _):
            for h in range(halves):
                zsend[exchange, 0, h, p] = black[h, p, pl.ds(PAD + depth - 2, 2), :]
                zsend[exchange, 1, h, p] = black[h, p, pl.ds(PAD, 2), :]
                if exchange == 0:
                    for side, at in ((0, PAD + depth - 1), (1, PAD)):
                        zsend[PASSES, side, h, p, pl.ds(0, 1), :] = red[h, p, pl.ds(at, 1), :]
                        zsend[PASSES, side, h, p, pl.ds(1, 1), :] = source[RED, h, p, pl.ds(at, 1), :]

        for p in range(pairs):
            gather(p, 0)

    def take_z(exchange):
        for side in range(2):
            @pl.when((has_prev, has_next)[side])
            def _():
                for copy in zmoves(exchange, side):
                    copy.wait_recv()
                two = pl.ds((PAD - 2, PAD + depth)[side], 2)
                one = pl.ds((PAD - 1, PAD + depth)[side], 1)
                for h in range(halves):
                    for p in range(pairs):
                        black[h, p, two, :] = zrecv[exchange, side, h, p]
                        if exchange == 0:
                            red[h, p, one, :] = zrecv[PASSES, side, h, p, pl.ds(0, 1), :]
                            source[RED, h, p, one, :] = zrecv[PASSES, side, h, p, pl.ds(1, 1), :]
                    for face in range(2):
                        black[h, halo_black(exchange)[face], two, :] = crecv[exchange, side, face, h]

    def loop(low, high, body, unroll=UNROLL):
        odd = (high - low) % unroll

        def several(n, _):
            for step in range(unroll):
                body(low + odd + n * unroll + step)
            return 0

        for p in range(low, low + odd):
            body(p)
        lax.fori_loop(0, (high - low) // unroll, several, 0)

    inside = range(1, tiles - 1)
    core = range(2, tiles - 2)
    rims = (0, tiles - 1)

    def red_inside(p):
        update(RED, p, p, p - 1, p + 1, inside)

    def finish(p, before, after, which, first):
        mask = parity_mask()
        sums = [[nothing if first else partial[h, 2 * p + side] for side in range(2)] for h in range(halves)]
        for tile, result in fresh_tiles(BLACK, p, p, before, after, which):
            for h, (value, near) in enumerate(result):
                for side in range(2):
                    plane = lax.select(mask, near, value) if side == 0 else lax.select(mask, value, near)
                    full[2 * p + 1 + side, pl.ds(8 * tile, 8), pl.ds(LANES * h, LANES)] = plane
                    sums[h][side] = sums[h][side] + plane
        for h in range(halves):
            for side in range(2):
                partial[h, 2 * p + side] = sums[h][side]

    def edges(sweep, piece):
        low, high = halo_black(sweep)
        on_j(sweep, piece, lambda copy: copy.wait_recv())
        if sweep == 0:
            unmix(piece)
        cut = first_tiles(sweep)
        own_tiles = range(-1, cut) if piece == 0 else range(cut, tiles + 1)
        halo_tiles = range(cut - 1) if piece == 0 else range(cut - 1, tiles)
        for side in range(2):
            p, before, after = ((0, low, 1), (pairs - 1, pairs - 2, high))[side]
            update(RED, p, p, before, after, own_tiles)
            p, near, before, after = ((halo[0], low, low, 0), (halo[1], high, pairs - 1, high))[side]
            update(RED, p, near, before, after, halo_tiles)
        for p, before, after in ((0, halo[0], 1), (pairs - 1, pairs - 2, halo[1])):
            if sweep < PASSES - 1:
                update(BLACK, p, p, before, after, halo_tiles)
            else:
                finish(p, before, after, halo_tiles, piece == 0)
        on_j(sweep + 1, piece, lambda copy: copy.start())

    for batch in ends:
        for copy in batch:
            copy.wait()
    loop(0, pairs, lambda p: prepare(p, rims))
    send_z(0)
    for p in (0, pairs - 1):
        for copy in pair_loads(p):
            copy.wait()
        prepare(p, inside)
    for side in range(2):
        mix(side)
    pl.semaphore_wait(barrier, 2 + 3 * (slabs - 1))
    on_z(0, lambda copy: copy.start())
    for piece in range(2):
        on_j(0, piece, lambda copy: copy.start())

    def arrive(p):
        for copy in pair_loads(p):
            copy.wait()
        prepare(p, inside)

    arrive(1)

    def arrive_and_update(p):
        arrive(p)
        red_inside(p - 1)

    loop(2, pairs - 1, arrive_and_update, 1)
    red_inside(pairs - 2)

    for sweep in range(PASSES):
        take_z(sweep)
        loop(1, pairs - 1, lambda p: update(RED, p, p, p - 1, p + 1, (-1, 0, tiles - 1, tiles)))
        for piece in range(2):
            on_j(sweep, piece, lambda copy: copy.wait_send())
        for piece in range(2):
            edges(sweep, piece)
        if sweep < PASSES - 1:
            loop(1, pairs - 1, lambda p: update(BLACK, p, p, p - 1, p + 1, rims))
            send_z(sweep + 1)
            on_z(sweep + 1, lambda copy: copy.start())
            loop(1, pairs - 1, lambda p: update(BLACK, p, p, p - 1, p + 1, inside))
            on_z(sweep, lambda copy: copy.wait_send())
            loop(1, pairs - 1, red_inside)
        if sweep == PASSES - 2:
            loop(2, pairs - 2, lambda p: finish(p, p - 1, p + 1, core, True))

    for p in (1, pairs - 2):
        finish(p, p - 1, p + 1, range(tiles), True)
    loop(2, pairs - 2, lambda p: finish(p, p - 1, p + 1, (0, 1, tiles - 2, tiles - 1), False))

    def add_up(group, _):
        for n in range(8):
            for h in range(halves):
                total[h, pl.ds(8 * group + n, 1), :] = jnp.sum(partial[h, 8 * group + n], axis=0, keepdims=True)
        return 0

    lax.fori_loop(0, sectors // 8, add_up, 0)
    for h in range(halves):
        edge[0, h] = total[h, pl.ds(sectors - 1, 1), :]
        edge[1, h] = total[h, pl.ds(0, 1), :]

    def tcopies(step):
        lower = lax.rem(slab + slabs - step, slabs)
        return [
            pltpu.make_async_remote_copy(
                src_ref=total,
                dst_ref=total_recv.at[step - 1],
                send_sem=tsend_sem.at[step - 1],
                recv_sem=trecv_sem.at[step - 1],
                device_id={"gz": lower},
                device_id_type=MESH,
            )
        ] + [
            pltpu.make_async_remote_copy(
                src_ref=edge.at[face],
                dst_ref=edge_recv.at[step - 1, face],
                send_sem=esend_sem.at[step - 1, face],
                recv_sem=erecv_sem.at[step - 1, face],
                device_id={"gz": lower, "phi": (right, left)[face]},
                device_id_type=MESH,
            )
            for face in range(2)
        ]

    for step in range(1, slabs):
        @pl.when(slab >= step)
        def _():
            for copy in tcopies(step):
                copy.start()

    carry[...] = jnp.zeros(carry.shape, jnp.float32)
    on_z(PASSES - 1, lambda copy: copy.wait_send())
    for step in range(1, slabs):
        @pl.when(slab + step < slabs)
        def _():
            for copy in tcopies(step):
                copy.wait_recv()
            for h in range(halves):
                carry[h, pl.ds(1, sectors), :] = carry[h, pl.ds(1, sectors), :] + total_recv[step - 1, h]
                for face, at in ((0, 0), (1, sectors + 1)):
                    carry[h, pl.ds(at, 1), :] = carry[h, pl.ds(at, 1), :] + edge_recv[step - 1, face, h]

    for piece in range(2):
        on_j(PASSES, piece, lambda copy: copy.wait())
    for step in range(1, slabs):
        @pl.when(slab >= step)
        def _():
            for copy in tcopies(step):
                copy.wait_send()


def drift_kernel(
    rings, full, carry, potential, shift_r, shift_phi,
    coef, runs, ones, twos, sums, out_r, out_phi, pot_sem, out_sem,
):
    halves = runs.shape[1]
    sectors = full.shape[0] - 2
    depth = full.shape[1]
    pairs = sectors // 2
    tiles = depth // 8
    row = lax.broadcasted_iota(jnp.int32, (8, LANES), 0)
    lane = lax.broadcasted_iota(jnp.int32, (8, LANES), 1)

    pot_copy = pltpu.make_async_copy(full.at[pl.ds(1, sectors)], potential, pot_sem)
    pot_copy.start()
    drift = 1.0 / (1.09 * 32.0)
    for h in range(halves):
        outward, inward, _, _, step = geometry(h, LANES * halves, sectors * rings)
        coef[0, h] = jnp.where(outward > 0.0, -0.5 * drift, 0.0)
        coef[1, h] = jnp.where(inward > 0.0, 0.5 * drift, 0.0)
        coef[2, h] = -0.5 * drift / step
        coef[3, h] = 0.3 * (-0.5 * drift / step)

    def out_copies(pair):
        planes = pl.ds(2 * pair, 2)
        return [
            pltpu.make_async_copy(src.at[planes], dst.at[planes], out_sem.at[n, pair])
            for n, (src, dst) in enumerate(((out_r, shift_r), (out_phi, shift_phi)))
        ]

    def integrate(plane, slot):
        for h in range(halves):
            after = jnp.broadcast_to(carry[h, pl.ds(plane, 1), :], (8, LANES))
            run = jnp.where(row == 0, after, 0.0)
            for ref in (runs, ones, twos):
                ref[slot, h, pl.ds(depth, 8), :] = run
            for tile in range(tiles - 1, -1, -1):
                run = run + full[plane, pl.ds(8 * tile, 8), pl.ds(LANES * h, LANES)]
                runs[slot, h, pl.ds(8 * tile, 8), :] = run
        for h in range(halves):
            for src, dst, hop in ((runs, ones, 1), (ones, twos, 2)):
                for tile in range(tiles - 1, -1, -1):
                    at = 8 * tile
                    dst[slot, h, pl.ds(at, 8), :] = src[slot, h, pl.ds(at, 8), :] + src[slot, h, pl.ds(at + hop, 8), :]
            for tile in range(tiles - 1, -1, -1):
                at = 8 * tile
                sums[plane, h, pl.ds(at, 8), :] = twos[slot, h, pl.ds(at, 8), :] + twos[slot, h, pl.ds(at + 4, 8), :]

    def combine(plane):
        for tile in range(tiles):
            rows = pl.ds(8 * tile, 8)
            outer, inner = beside([sums[plane, h, rows, :] for h in range(halves)], lane)
            for h in range(halves):
                lanes = pl.ds(LANES * h, LANES)
                along_r = coef[0, h] * outer[h] + coef[1, h] * inner[h]
                across = sums[plane + 1, h, rows, :] - sums[plane - 1, h, rows, :]
                out_r[plane - 1, rows, lanes] = along_r + coef[3, h] * across
                out_phi[plane - 1, rows, lanes] = coef[2, h] * across - 0.3 * along_r

    def emit(pair):
        combine(2 * pair + 1)
        combine(2 * pair + 2)
        for copy in out_copies(pair):
            copy.start()

    for plane in range(4):
        integrate(plane, plane % 2)

    def body(g, _):
        integrate(2 * g, 0)
        integrate(2 * g + 1, 1)
        emit(g - 2)
        return 0

    lax.fori_loop(2, pairs + 1, body, 0)
    emit(pairs - 1)

    def drain(pair, _):
        for copy in out_copies(pair):
            copy.wait()
        return 0

    lax.fori_loop(0, pairs, drain, 0)
    pot_copy.wait()


def local(slabs, rings, potential_in, charge, cell_kind):
    sectors, depth, radial = potential_in.shape
    pairs, halves = sectors // 2, radial // LANES
    tall = depth + 2 * PAD
    any_spec = pl.BlockSpec(memory_space=pl.ANY)
    vmem_spec = pl.BlockSpec(memory_space=pltpu.VMEM)
    f32 = jnp.float32
    dma = pltpu.SemaphoreType.DMA
    full, carry = pl.pallas_call(
        functools.partial(relax_kernel, slabs, rings),
        out_shape=(
            pltpu.VMEM((sectors + 2, depth, radial), f32),
            pltpu.VMEM((halves, sectors + 2, LANES), f32),
        ),
        in_specs=[any_spec] * 3,
        out_specs=(vmem_spec, vmem_spec),
        scratch_shapes=[
            pltpu.VMEM((4, halves, 8, LANES), f32),
            pltpu.VMEM((sectors, depth, radial), f32),
            pltpu.VMEM((sectors, depth, radial), f32),
            pltpu.VMEM((sectors, depth, radial), jnp.int32),
            pltpu.VMEM((halves, pairs + 2, tall, LANES), f32),
            pltpu.VMEM((halves, pairs + 2 * PASSES, tall, LANES), f32),
            pltpu.VMEM((2, halves, pairs + 2, tall, LANES), f32),
            pltpu.VMEM((2, halves, depth, LANES), f32),
            pltpu.VMEM((PASSES + 1, 2, halves, pairs, 2, LANES), f32),
            pltpu.VMEM((PASSES + 1, 2, halves, pairs, 2, LANES), f32),
            pltpu.VMEM((PASSES, 2, 2, halves, 2, LANES), f32),
            pltpu.VMEM((halves, sectors, 8, LANES), f32),
            pltpu.VMEM((halves, sectors, LANES), f32),
            pltpu.VMEM((slabs - 1, halves, sectors, LANES), f32),
            pltpu.VMEM((2, halves, 1, LANES), f32),
            pltpu.VMEM((slabs - 1, 2, halves, 1, LANES), f32),
            dma((pairs + 2, 3)),
            dma((PASSES + 1, 2, 2, 2)),
            dma((PASSES + 1, 2, 2, 2)),
            dma((PASSES + 1, 2)),
            dma((PASSES + 1, 2)),
            dma((PASSES, 2, 2)),
            dma((PASSES, 2, 2)),
            dma((slabs - 1,)),
            dma((slabs - 1,)),
            dma((slabs - 1, 2)),
            dma((slabs - 1, 2)),
        ],
        compiler_params=pltpu.CompilerParams(
            collective_id=0, has_side_effects=True, vmem_limit_bytes=48 * 2**20
        ),
    )(potential_in, charge, cell_kind)

    full = pltpu.with_memory_space_constraint(full, pltpu.VMEM)
    carry = pltpu.with_memory_space_constraint(carry, pltpu.VMEM)
    block = jax.ShapeDtypeStruct((sectors, depth, radial), f32)
    return pl.pallas_call(
        functools.partial(drift_kernel, rings),
        out_shape=(block, block, block),
        in_specs=[vmem_spec, vmem_spec],
        out_specs=(any_spec,) * 3,
        scratch_shapes=[
            pltpu.VMEM((4, halves, 8, LANES), f32),
            pltpu.VMEM((2, halves, depth + 8, LANES), f32),
            pltpu.VMEM((2, halves, depth + 8, LANES), f32),
            pltpu.VMEM((2, halves, depth + 8, LANES), f32),
            pltpu.VMEM((sectors + 2, halves, depth, LANES), f32),
            pltpu.VMEM((sectors, depth, radial), f32),
            pltpu.VMEM((sectors, depth, radial), f32),
            dma,
            dma((2, pairs)),
        ],
        compiler_params=pltpu.CompilerParams(vmem_limit_bytes=24 * 2**20),
    )(full, carry)


def solution(mesh):
    spec = P("phi", "gz", None)
    body = functools.partial(local, mesh.shape["gz"], mesh.shape["phi"])
    return jax.shard_map(body, mesh=mesh, in_specs=(spec,) * 3, out_specs=(spec,) * 3, check_vma=False)
```

```python
import functools
import math

import jax
import jax.numpy as jnp
from jax import lax
from jax.experimental import pallas as pl
from jax.experimental.pallas import tpu as pltpu
from jax.sharding import PartitionSpec as P

PASSES = 3
RELAX = 1.5
FIXED = 1e30
MESH = pl.DeviceIdType.MESH
PAD = 16
LANES = 128
RED, BLACK = 0, 1
UNROLL = 2


def parity_mask():
    row = lax.broadcasted_iota(jnp.int32, (8, LANES), 0)
    lane = lax.broadcasted_iota(jnp.int32, (8, LANES), 1)
    return ((row + lane) & 1) == 0


def beside(halves, lane):
    ahead = [pltpu.roll(x, LANES - 1, axis=1) for x in halves]
    behind = [pltpu.roll(x, 1, axis=1) for x in halves]
    last = len(halves) - 1
    outer = [ahead[h] if h == last else lax.select(lane == LANES - 1, ahead[h + 1], ahead[h]) for h in range(last + 1)]
    inner = [behind[h] if h == 0 else lax.select(lane == 0, behind[h - 1], behind[h]) for h in range(last + 1)]
    return outer, inner


def geometry(half, radial, sectors):
    cell = lax.broadcasted_iota(jnp.int32, (8, LANES), 1) + LANES * half
    radius = radial * 0.5 + cell.astype(jnp.float32) + 0.5
    step = radius * (2.0 * math.pi / sectors)
    around = 1.0 / (step * step)
    outward = jnp.where(cell < radial - 1, 1.0 + 0.5 / radius, 0.0)
    inward = jnp.where(cell > 0, 1.0 - 0.5 / radius, 0.0)
    return outward, inward, around, 4.0 + 2.0 * around, step


def relax_kernel(
    slabs, rings, pot, chg, kind, full, carry,
    coef, pot_in, chg_in, kind_in, red, black, source, mixed, zsend, zrecv, crecv,
    partial, total, total_recv, edge, edge_recv,
    load_sem, jsend_sem, jrecv_sem, zsend_sem, zrecv_sem, csend_sem, crecv_sem,
    tsend_sem, trecv_sem, esend_sem, erecv_sem,
):
    halves = red.shape[0]
    sectors, depth, radial = pot_in.shape
    pairs = sectors // 2
    tiles = depth // 8
    slab = lax.axis_index("gz")
    ring = lax.axis_index("phi")
    right, left = lax.rem(ring + 1, rings), lax.rem(ring + rings - 1, rings)
    has_next, has_prev = slab < slabs - 1, slab > 0
    halo = (pairs, pairs + 1)

    def loads(slot, planes, rows):
        return [
            pltpu.make_async_copy(src.at[planes, rows], dst.at[planes, rows], load_sem.at[slot, n])
            for n, (src, dst) in enumerate(((pot, pot_in), (chg, chg_in), (kind, kind_in)))
        ]

    every, middle = pl.ds(0, sectors), pl.ds(8, depth - 16)
    ends = [loads(pairs, every, pl.ds(0, 8)), loads(pairs + 1, every, pl.ds(depth - 8, 8))]

    def pair_loads(p):
        return loads(p, pl.ds(2 * p, 2), middle)

    for batch in ends:
        for copy in batch:
            copy.start()
    for p in (0, pairs - 1):
        for copy in pair_loads(p):
            copy.start()

    def start_pair(p, _):
        for copy in pair_loads(p):
            copy.start()
        return 0

    lax.fori_loop(1, pairs - 1, start_pair, 0)

    barrier = pltpu.get_barrier_semaphore()
    for neighbour in (left, right):
        pl.semaphore_signal(barrier, inc=1, device_id={"phi": neighbour}, device_id_type=MESH)
    for step in range(1, slabs):
        peer = lax.rem(slab + step, slabs)
        for column in (left, ring, right):
            pl.semaphore_signal(barrier, inc=1, device_id={"gz": peer, "phi": column}, device_id_type=MESH)

    for h in range(halves):
        outward, inward, around_i, diag, _ = geometry(h, radial, sectors * rings)
        for n, values in enumerate((outward, inward, around_i, RELAX / diag)):
            coef[n, h] = values

    nothing = jnp.zeros((8, LANES), jnp.float32)
    held = jnp.full((8, LANES), FIXED, jnp.float32)

    def clear(p, _):
        for h in range(halves):
            for rows in (pl.ds(PAD - 8, 8), pl.ds(PAD + depth, 8)):
                black[h, p, rows, :] = nothing
        return 0

    def clear_own(p, _):
        for h in range(halves):
            for rows in (pl.ds(PAD - 8, 8), pl.ds(PAD + depth, 8)):
                red[h, p, rows, :] = nothing
                source[RED, h, p, rows, :] = held
        return 0

    lax.fori_loop(0, black.shape[1], clear, 0)
    lax.fori_loop(0, pairs, clear_own, 0)

    def prepare(p, which):
        mask = parity_mask()
        for tile in which:
            rows, out = pl.ds(8 * tile, 8), pl.ds(PAD + 8 * tile, 8)
            for h in range(halves):
                lanes = pl.ds(LANES * h, LANES)
                plane, charges = [], []
                for side in range(2):
                    what = kind_in[2 * p + side, rows, lanes]
                    plane.append(lax.select(what == 1, nothing, pot_in[2 * p + side, rows, lanes]))
                    charges.append(lax.select(what == 0, chg_in[2 * p + side, rows, lanes], held))
                red[h, p, out, :] = lax.select(mask, plane[0], plane[1])
                black[h, p, out, :] = lax.select(mask, plane[1], plane[0])
                source[RED, h, p, out, :] = lax.select(mask, charges[0], charges[1])
                source[BLACK, h, p, out, :] = lax.select(mask, charges[1], charges[0])

    def fresh_tiles(color, p, near, before, after, which):
        own, other = (red, black) if color == RED else (black, red)
        mask = parity_mask()
        lane = lax.broadcasted_iota(jnp.int32, (8, LANES), 1)
        first, second = (before, after) if color == RED else (after, before)
        factor = [[coef[n, h] for n in range(4)] for h in range(halves)]
        for tile in which:
            at = PAD + 8 * tile
            rows = pl.ds(at, 8)
            here = [other[h, near, rows, :] for h in range(halves)]
            outer, inner = beside(here, lane)
            result = []
            for h in range(halves):
                out_c, in_c, around_c, scale = factor[h]
                around = here[h] + lax.select(mask, other[h, first, rows, :], other[h, second, rows, :])
                along = other[h, near, pl.ds(at - 1, 8), :] + other[h, near, pl.ds(at + 1, 8), :]
                put = source[color, h, p, rows, :]
                old = own[h, p, rows, :]
                gathered = (put + along) + (out_c * outer[h] + in_c * inner[h]) + around_c * around
                fresh = scale * gathered - (RELAX - 1.0) * old
                result.append((lax.select(put < 0.5 * FIXED, fresh, old), here[h]))
            yield tile, result

    def update(color, p, near, before, after, which):
        own = red if color == RED else black
        for tile, result in fresh_tiles(color, p, near, before, after, which):
            for h, (value, _) in enumerate(result):
                own[h, p, pl.ds(PAD + 8 * tile, 8), :] = value

    def halo_black(exchange):
        return pairs + 2 * exchange, pairs + 2 * exchange + 1

    def outer_tiles(exchange):
        return tiles // 4 + 2 - exchange

    def spans(cut, piece):
        return [(0, cut), (tiles - cut, tiles)] if piece == 0 else [(cut, tiles - cut)]

    def jcopies(exchange, side, piece):
        moves = []
        for low, high in spans(outer_tiles(exchange), piece):
            plain = pl.ds(8 * low, 8 * (high - low))
            rows = pl.ds(PAD + 8 * low, 8 * (high - low))
            if exchange == PASSES:
                moves.append((full.at[(sectors, 1)[side], plain], full.at[(0, sectors + 1)[side], plain]))
                continue
            edge_pair = (pairs - 1, 0)[side]
            moves.append((black.at[:, edge_pair, rows], black.at[:, halo_black(exchange)[side], rows]))
            if exchange == 0:
                moves.append((mixed.at[side, :, plain], red.at[:, halo[side], rows]))
        return [
            pltpu.make_async_remote_copy(
                src_ref=src,
                dst_ref=dst,
                send_sem=jsend_sem.at[exchange, n, side, piece],
                recv_sem=jrecv_sem.at[exchange, n, side, piece],
                device_id={"phi": (right, left)[side]},
                device_id_type=MESH,
            )
            for n, (src, dst) in enumerate(moves)
        ]

    def on_j(exchange, piece, act):
        for side in range(2):
            for copy in jcopies(exchange, side, piece):
                act(copy)

    def mix(side):
        p = (pairs - 1, 0)[side]
        mask = parity_mask()
        for tile in range(tiles):
            rows = pl.ds(PAD + 8 * tile, 8)
            for h in range(halves):
                values, charges = red[h, p, rows, :], pltpu.roll(source[RED, h, p, rows, :], 1, axis=1)
                both = (charges, values) if side == 0 else (values, charges)
                mixed[side, h, pl.ds(8 * tile, 8), :] = lax.select(mask, *both)

    def unmix(piece):
        for low, high in spans(outer_tiles(0), piece):
            for tile in range(low, high):
                rows = pl.ds(PAD + 8 * tile, 8)
                for side in range(2):
                    for h in range(halves):
                        source[RED, h, halo[side], rows, :] = pltpu.roll(red[h, halo[side], rows, :], LANES - 1, axis=1)

    def zcopy(slot, side):
        return pltpu.make_async_remote_copy(
            src_ref=zsend.at[slot, side],
            dst_ref=zrecv.at[slot, side],
            send_sem=zsend_sem.at[slot, side],
            recv_sem=zrecv_sem.at[slot, side],
            device_id={"gz": (lax.rem(slab + 1, slabs), lax.rem(slab + slabs - 1, slabs))[side]},
            device_id_type=MESH,
        )

    def ccopy(exchange, side, face):
        return pltpu.make_async_remote_copy(
            src_ref=zsend.at[exchange, side, :, (pairs - 1, 0)[face]],
            dst_ref=crecv.at[exchange, side, face],
            send_sem=csend_sem.at[exchange, side, face],
            recv_sem=crecv_sem.at[exchange, side, face],
            device_id={
                "gz": (lax.rem(slab + 1, slabs), lax.rem(slab + slabs - 1, slabs))[side],
                "phi": (right, left)[face],
            },
            device_id_type=MESH,
        )

    def zmoves(exchange, side):
        rows = [zcopy(exchange, side)] + ([zcopy(PASSES, side)] if exchange == 0 else [])
        return [ccopy(exchange, side, face) for face in range(2)] + rows

    def on_z(exchange, act):
        for side in range(2):
            @pl.when((has_next, has_prev)[side])
            def _():
                for copy in zmoves(exchange, side):
                    act(copy)

    def send_z(exchange):
        def gather(p, _):
            for h in range(halves):
                zsend[exchange, 0, h, p] = black[h, p, pl.ds(PAD + depth - 2, 2), :]
                zsend[exchange, 1, h, p] = black[h, p, pl.ds(PAD, 2), :]
                if exchange == 0:
                    for side, at in ((0, PAD + depth - 1), (1, PAD)):
                        zsend[PASSES, side, h, p, pl.ds(0, 1), :] = red[h, p, pl.ds(at, 1), :]
                        zsend[PASSES, side, h, p, pl.ds(1, 1), :] = source[RED, h, p, pl.ds(at, 1), :]

        for p in range(pairs):
            gather(p, 0)

    def take_z(exchange):
        for side in range(2):
            @pl.when((has_prev, has_next)[side])
            def _():
                for copy in zmoves(exchange, side):
                    copy.wait_recv()
                two = pl.ds((PAD - 2, PAD + depth)[side], 2)
                one = pl.ds((PAD - 1, PAD + depth)[side], 1)
                for h in range(halves):
                    for p in range(pairs):
                        black[h, p, two, :] = zrecv[exchange, side, h, p]
                        if exchange == 0:
                            red[h, p, one, :] = zrecv[PASSES, side, h, p, pl.ds(0, 1), :]
                            source[RED, h, p, one, :] = zrecv[PASSES, side, h, p, pl.ds(1, 1), :]
                    for face in range(2):
                        black[h, halo_black(exchange)[face], two, :] = crecv[exchange, side, face, h]

    def loop(low, high, body, unroll=UNROLL):
        odd = (high - low) % unroll if unroll < high - low else high - low

        def several(n, _):
            for step in range(unroll):
                body(low + odd + n * unroll + step)
            return 0

        for p in range(low, low + odd):
            body(p)
        if odd < high - low:
            lax.fori_loop(0, (high - low) // unroll, several, 0)

    inside = range(1, tiles - 1)
    core = range(2, tiles - 2)
    rims = (0, tiles - 1)

    def red_inside(p):
        update(RED, p, p, p - 1, p + 1, inside)

    def finish(p, before, after, which, first):
        mask = parity_mask()
        sums = [[nothing if first else partial[h, 2 * p + side] for side in range(2)] for h in range(halves)]
        for tile, result in fresh_tiles(BLACK, p, p, before, after, which):
            for h, (value, near) in enumerate(result):
                for side in range(2):
                    plane = lax.select(mask, near, value) if side == 0 else lax.select(mask, value, near)
                    full[2 * p + 1 + side, pl.ds(8 * tile, 8), pl.ds(LANES * h, LANES)] = plane
                    sums[h][side] = sums[h][side] + plane
        for h in range(halves):
            for side in range(2):
                partial[h, 2 * p + side] = sums[h][side]

    def edges(sweep, piece):
        low, high = halo_black(sweep)
        on_j(sweep, piece, lambda copy: copy.wait_recv())
        if sweep == 0:
            unmix(piece)
        cut = outer_tiles(sweep)
        halo_tiles = [tile for low, high in spans(cut - 1, piece) for tile in range(low, high)]
        own_tiles = [tile for low, high in spans(cut, piece) for tile in range(low, high)]
        if piece == 0:
            own_tiles = [-1, *own_tiles, tiles]
        for side in range(2):
            p, before, after = ((0, low, 1), (pairs - 1, pairs - 2, high))[side]
            update(RED, p, p, before, after, own_tiles)
            p, near, before, after = ((halo[0], low, low, 0), (halo[1], high, pairs - 1, high))[side]
            update(RED, p, near, before, after, halo_tiles)
        for p, before, after in ((0, halo[0], 1), (pairs - 1, pairs - 2, halo[1])):
            if sweep < PASSES - 1:
                update(BLACK, p, p, before, after, halo_tiles)
            else:
                finish(p, before, after, halo_tiles, piece == 0)
        on_j(sweep + 1, piece, lambda copy: copy.start())

    for batch in ends:
        for copy in batch:
            copy.wait()
    loop(0, pairs, lambda p: prepare(p, rims))
    send_z(0)
    for p in (0, pairs - 1):
        for copy in pair_loads(p):
            copy.wait()
        prepare(p, inside)
    for side in range(2):
        mix(side)
    pl.semaphore_wait(barrier, 2 + 3 * (slabs - 1))
    on_z(0, lambda copy: copy.start())
    for piece in range(2):
        on_j(0, piece, lambda copy: copy.start())

    def arrive(p):
        for copy in pair_loads(p):
            copy.wait()
        prepare(p, inside)

    arrive(1)

    def arrive_and_update(p):
        arrive(p)
        red_inside(p - 1)

    loop(2, pairs - 1, arrive_and_update, 1)
    red_inside(pairs - 2)

    def black_rims(p):
        update(BLACK, p, p, p - 1, p + 1, rims)

    for sweep in range(PASSES):
        more = sweep < PASSES - 1
        take_z(sweep)
        loop(1, pairs - 1, lambda p: update(RED, p, p, p - 1, p + 1, (-1, 0, tiles - 1, tiles)), pairs - 2)
        if more:
            loop(2, pairs - 2, black_rims, pairs - 4)
        for piece in range(2):
            on_j(sweep, piece, lambda copy: copy.wait_send())
        edges(sweep, 0)
        if more:
            for p in (1, pairs - 2):
                black_rims(p)
            send_z(sweep + 1)
            on_z(sweep + 1, lambda copy: copy.start())
        edges(sweep, 1)
        if more:
            loop(1, pairs - 1, lambda p: update(BLACK, p, p, p - 1, p + 1, inside))
            on_z(sweep, lambda copy: copy.wait_send())
            loop(1, pairs - 1, red_inside)
        if sweep == PASSES - 2:
            loop(2, pairs - 2, lambda p: finish(p, p - 1, p + 1, core, True))

    for p in (1, pairs - 2):
        finish(p, p - 1, p + 1, range(tiles), True)
    loop(2, pairs - 2, lambda p: finish(p, p - 1, p + 1, (0, 1, tiles - 2, tiles - 1), False), pairs - 4)

    def add_up(group, _):
        for n in range(8):
            for h in range(halves):
                total[h, pl.ds(8 * group + n, 1), :] = jnp.sum(partial[h, 8 * group + n], axis=0, keepdims=True)
        return 0

    lax.fori_loop(0, sectors // 8, add_up, 0)
    for h in range(halves):
        edge[0, h] = total[h, pl.ds(sectors - 1, 1), :]
        edge[1, h] = total[h, pl.ds(0, 1), :]

    def tcopies(step):
        lower = lax.rem(slab + slabs - step, slabs)
        return [
            pltpu.make_async_remote_copy(
                src_ref=total,
                dst_ref=total_recv.at[step - 1],
                send_sem=tsend_sem.at[step - 1],
                recv_sem=trecv_sem.at[step - 1],
                device_id={"gz": lower},
                device_id_type=MESH,
            )
        ] + [
            pltpu.make_async_remote_copy(
                src_ref=edge.at[face],
                dst_ref=edge_recv.at[step - 1, face],
                send_sem=esend_sem.at[step - 1, face],
                recv_sem=erecv_sem.at[step - 1, face],
                device_id={"gz": lower, "phi": (right, left)[face]},
                device_id_type=MESH,
            )
            for face in range(2)
        ]

    for step in range(1, slabs):
        @pl.when(slab >= step)
        def _():
            for copy in tcopies(step):
                copy.start()

    carry[...] = jnp.zeros(carry.shape, jnp.float32)
    on_z(PASSES - 1, lambda copy: copy.wait_send())
    for step in range(1, slabs):
        @pl.when(slab + step < slabs)
        def _():
            for copy in tcopies(step):
                copy.wait_recv()
            for h in range(halves):
                carry[h, pl.ds(1, sectors), :] = carry[h, pl.ds(1, sectors), :] + total_recv[step - 1, h]
                for face, at in ((0, 0), (1, sectors + 1)):
                    carry[h, pl.ds(at, 1), :] = carry[h, pl.ds(at, 1), :] + edge_recv[step - 1, face, h]

    for piece in range(2):
        on_j(PASSES, piece, lambda copy: copy.wait())
    for step in range(1, slabs):
        @pl.when(slab >= step)
        def _():
            for copy in tcopies(step):
                copy.wait_send()


def drift_kernel(
    rings, full, carry, potential, shift_r, shift_phi,
    coef, runs, ones, twos, sums, out_r, out_phi, pot_sem, out_sem,
):
    halves = runs.shape[1]
    sectors = full.shape[0] - 2
    depth = full.shape[1]
    pairs = sectors // 2
    tiles = depth // 8
    row = lax.broadcasted_iota(jnp.int32, (8, LANES), 0)
    lane = lax.broadcasted_iota(jnp.int32, (8, LANES), 1)

    pot_copy = pltpu.make_async_copy(full.at[pl.ds(1, sectors)], potential, pot_sem)
    pot_copy.start()
    drift = 1.0 / (1.09 * 32.0)
    for h in range(halves):
        outward, inward, _, _, step = geometry(h, LANES * halves, sectors * rings)
        coef[0, h] = jnp.where(outward > 0.0, -0.5 * drift, 0.0)
        coef[1, h] = jnp.where(inward > 0.0, 0.5 * drift, 0.0)
        coef[2, h] = -0.5 * drift / step
        coef[3, h] = 0.3 * (-0.5 * drift / step)

    def out_copies(pair):
        planes = pl.ds(2 * pair, 2)
        return [
            pltpu.make_async_copy(src.at[planes], dst.at[planes], out_sem.at[n, pair])
            for n, (src, dst) in enumerate(((out_r, shift_r), (out_phi, shift_phi)))
        ]

    def integrate(plane, slot):
        for h in range(halves):
            after = jnp.broadcast_to(carry[h, pl.ds(plane, 1), :], (8, LANES))
            run = jnp.where(row == 0, after, 0.0)
            for ref in (runs, ones, twos):
                ref[slot, h, pl.ds(depth, 8), :] = run
            for tile in range(tiles - 1, -1, -1):
                run = run + full[plane, pl.ds(8 * tile, 8), pl.ds(LANES * h, LANES)]
                runs[slot, h, pl.ds(8 * tile, 8), :] = run
        for h in range(halves):
            for src, dst, hop in ((runs, ones, 1), (ones, twos, 2)):
                for tile in range(tiles - 1, -1, -1):
                    at = 8 * tile
                    dst[slot, h, pl.ds(at, 8), :] = src[slot, h, pl.ds(at, 8), :] + src[slot, h, pl.ds(at + hop, 8), :]
            for tile in range(tiles - 1, -1, -1):
                at = 8 * tile
                sums[plane, h, pl.ds(at, 8), :] = twos[slot, h, pl.ds(at, 8), :] + twos[slot, h, pl.ds(at + 4, 8), :]

    def combine(plane):
        for tile in range(tiles):
            rows = pl.ds(8 * tile, 8)
            outer, inner = beside([sums[plane, h, rows, :] for h in range(halves)], lane)
            for h in range(halves):
                lanes = pl.ds(LANES * h, LANES)
                along_r = coef[0, h] * outer[h] + coef[1, h] * inner[h]
                across = sums[plane + 1, h, rows, :] - sums[plane - 1, h, rows, :]
                out_r[plane - 1, rows, lanes] = along_r + coef[3, h] * across
                out_phi[plane - 1, rows, lanes] = coef[2, h] * across - 0.3 * along_r

    def emit(pair):
        combine(2 * pair + 1)
        combine(2 * pair + 2)
        for copy in out_copies(pair):
            copy.start()

    for plane in range(4):
        integrate(plane, plane % 2)

    def body(g, _):
        integrate(2 * g, 0)
        integrate(2 * g + 1, 1)
        emit(g - 2)
        return 0

    lax.fori_loop(2, pairs + 1, body, 0)
    emit(pairs - 1)

    def drain(pair, _):
        for copy in out_copies(pair):
            copy.wait()
        return 0

    lax.fori_loop(0, pairs, drain, 0)
    pot_copy.wait()


def local(slabs, rings, potential_in, charge, cell_kind):
    sectors, depth, radial = potential_in.shape
    pairs, halves = sectors // 2, radial // LANES
    tall = depth + 2 * PAD
    any_spec = pl.BlockSpec(memory_space=pl.ANY)
    vmem_spec = pl.BlockSpec(memory_space=pltpu.VMEM)
    f32 = jnp.float32
    dma = pltpu.SemaphoreType.DMA
    full, carry = pl.pallas_call(
        functools.partial(relax_kernel, slabs, rings),
        out_shape=(
            pltpu.VMEM((sectors + 2, depth, radial), f32),
            pltpu.VMEM((halves, sectors + 2, LANES), f32),
        ),
        in_specs=[any_spec] * 3,
        out_specs=(vmem_spec, vmem_spec),
        scratch_shapes=[
            pltpu.VMEM((4, halves, 8, LANES), f32),
            pltpu.VMEM((sectors, depth, radial), f32),
            pltpu.VMEM((sectors, depth, radial), f32),
            pltpu.VMEM((sectors, depth, radial), jnp.int32),
            pltpu.VMEM((halves, pairs + 2, tall, LANES), f32),
            pltpu.VMEM((halves, pairs + 2 * PASSES, tall, LANES), f32),
            pltpu.VMEM((2, halves, pairs + 2, tall, LANES), f32),
            pltpu.VMEM((2, halves, depth, LANES), f32),
            pltpu.VMEM((PASSES + 1, 2, halves, pairs, 2, LANES), f32),
            pltpu.VMEM((PASSES + 1, 2, halves, pairs, 2, LANES), f32),
            pltpu.VMEM((PASSES, 2, 2, halves, 2, LANES), f32),
            pltpu.VMEM((halves, sectors, 8, LANES), f32),
            pltpu.VMEM((halves, sectors, LANES), f32),
            pltpu.VMEM((slabs - 1, halves, sectors, LANES), f32),
            pltpu.VMEM((2, halves, 1, LANES), f32),
            pltpu.VMEM((slabs - 1, 2, halves, 1, LANES), f32),
            dma((pairs + 2, 3)),
            dma((PASSES + 1, 4, 2, 2)),
            dma((PASSES + 1, 4, 2, 2)),
            dma((PASSES + 1, 2)),
            dma((PASSES + 1, 2)),
            dma((PASSES, 2, 2)),
            dma((PASSES, 2, 2)),
            dma((slabs - 1,)),
            dma((slabs - 1,)),
            dma((slabs - 1, 2)),
            dma((slabs - 1, 2)),
        ],
        compiler_params=pltpu.CompilerParams(
            collective_id=0, has_side_effects=True, vmem_limit_bytes=48 * 2**20
        ),
    )(potential_in, charge, cell_kind)

    full = pltpu.with_memory_space_constraint(full, pltpu.VMEM)
    carry = pltpu.with_memory_space_constraint(carry, pltpu.VMEM)
    block = jax.ShapeDtypeStruct((sectors, depth, radial), f32)
    return pl.pallas_call(
        functools.partial(drift_kernel, rings),
        out_shape=(block, block, block),
        in_specs=[vmem_spec, vmem_spec],
        out_specs=(any_spec,) * 3,
        scratch_shapes=[
            pltpu.VMEM((4, halves, 8, LANES), f32),
            pltpu.VMEM((2, halves, depth + 8, LANES), f32),
            pltpu.VMEM((2, halves, depth + 8, LANES), f32),
            pltpu.VMEM((2, halves, depth + 8, LANES), f32),
            pltpu.VMEM((sectors + 2, halves, depth, LANES), f32),
            pltpu.VMEM((sectors, depth, radial), f32),
            pltpu.VMEM((sectors, depth, radial), f32),
            dma,
            dma((2, pairs)),
        ],
        compiler_params=pltpu.CompilerParams(vmem_limit_bytes=24 * 2**20),
    )(full, carry)


def solution(mesh):
    spec = P("phi", "gz", None)
    body = functools.partial(local, mesh.shape["gz"], mesh.shape["phi"])
    return jax.shard_map(body, mesh=mesh, in_specs=(spec,) * 3, out_specs=(spec,) * 3, check_vma=False)
```

```python
import functools
import math

import jax
import jax.numpy as jnp
from jax import lax
from jax.experimental import pallas as pl
from jax.experimental.pallas import tpu as pltpu
from jax.sharding import PartitionSpec as P

PASSES = 3
RELAX = 1.5
FIXED = 1e30
MESH = pl.DeviceIdType.MESH
PAD = 16
LANES = 128
RED, BLACK = 0, 1
UNROLL = 2
STEPS = 3


def parity_mask():
    row = lax.broadcasted_iota(jnp.int32, (8, LANES), 0)
    lane = lax.broadcasted_iota(jnp.int32, (8, LANES), 1)
    return ((row + lane) & 1) == 0


def beside(halves, lane):
    ahead = [pltpu.roll(x, LANES - 1, axis=1) for x in halves]
    behind = [pltpu.roll(x, 1, axis=1) for x in halves]
    last = len(halves) - 1
    outer = [ahead[h] if h == last else lax.select(lane == LANES - 1, ahead[h + 1], ahead[h]) for h in range(last + 1)]
    inner = [behind[h] if h == 0 else lax.select(lane == 0, behind[h - 1], behind[h]) for h in range(last + 1)]
    return outer, inner


def geometry(half, radial, sectors):
    cell = lax.broadcasted_iota(jnp.int32, (8, LANES), 1) + LANES * half
    radius = radial * 0.5 + cell.astype(jnp.float32) + 0.5
    step = radius * (2.0 * math.pi / sectors)
    around = 1.0 / (step * step)
    outward = jnp.where(cell < radial - 1, 1.0 + 0.5 / radius, 0.0)
    inward = jnp.where(cell > 0, 1.0 - 0.5 / radius, 0.0)
    return outward, inward, around, 4.0 + 2.0 * around, step


def relax_kernel(
    slabs, rings, pot, chg, kind, full, carry,
    coef, pot_in, chg_in, kind_in, red, black, source, mixed, zsend, zrecv, crecv,
    partial, total, total_recv, edge, edge_recv,
    load_sem, jsend_sem, jrecv_sem, zsend_sem, zrecv_sem, csend_sem, crecv_sem,
    tsend_sem, trecv_sem, esend_sem, erecv_sem,
):
    halves = red.shape[0]
    sectors, depth, radial = pot_in.shape
    pairs = sectors // 2
    tiles = depth // 8
    slab = lax.axis_index("gz")
    ring = lax.axis_index("phi")
    right, left = lax.rem(ring + 1, rings), lax.rem(ring + rings - 1, rings)
    has_next, has_prev = slab < slabs - 1, slab > 0
    halo = (pairs, pairs + 1)

    def loads(slot, planes, rows):
        return [
            pltpu.make_async_copy(src.at[planes, rows], dst.at[planes, rows], load_sem.at[slot, n])
            for n, (src, dst) in enumerate(((pot, pot_in), (chg, chg_in), (kind, kind_in)))
        ]

    every, middle = pl.ds(0, sectors), pl.ds(8, depth - 16)
    ends = [loads(pairs, every, pl.ds(0, 8)), loads(pairs + 1, every, pl.ds(depth - 8, 8))]

    def pair_loads(p):
        return loads(p, pl.ds(2 * p, 2), middle)

    for batch in ends:
        for copy in batch:
            copy.start()
    for p in (0, pairs - 1):
        for copy in pair_loads(p):
            copy.start()

    def start_pair(p, _):
        for copy in pair_loads(p):
            copy.start()
        return 0

    lax.fori_loop(1, pairs - 1, start_pair, 0)

    barrier = pltpu.get_barrier_semaphore()
    for neighbour in (left, right):
        pl.semaphore_signal(barrier, inc=1, device_id={"phi": neighbour}, device_id_type=MESH)
    for step in range(1, slabs):
        peer = lax.rem(slab + step, slabs)
        for column in (left, ring, right):
            pl.semaphore_signal(barrier, inc=1, device_id={"gz": peer, "phi": column}, device_id_type=MESH)

    for h in range(halves):
        outward, inward, around_i, diag, _ = geometry(h, radial, sectors * rings)
        for n, values in enumerate((outward, inward, around_i, RELAX / diag)):
            coef[n, h] = values

    nothing = jnp.zeros((8, LANES), jnp.float32)
    held = jnp.full((8, LANES), FIXED, jnp.float32)

    def clear(p, _):
        for h in range(halves):
            for rows in (pl.ds(PAD - 8, 8), pl.ds(PAD + depth, 8)):
                black[h, p, rows, :] = nothing
        return 0

    def clear_own(p, _):
        for h in range(halves):
            for rows in (pl.ds(PAD - 8, 8), pl.ds(PAD + depth, 8)):
                red[h, p, rows, :] = nothing
                source[RED, h, p, rows, :] = held
        return 0

    lax.fori_loop(0, black.shape[1], clear, 0)
    lax.fori_loop(0, pairs, clear_own, 0)

    def prepare(p, which):
        mask = parity_mask()
        for tile in which:
            rows, out = pl.ds(8 * tile, 8), pl.ds(PAD + 8 * tile, 8)
            for h in range(halves):
                lanes = pl.ds(LANES * h, LANES)
                plane, charges = [], []
                for side in range(2):
                    what = kind_in[2 * p + side, rows, lanes]
                    plane.append(lax.select(what == 1, nothing, pot_in[2 * p + side, rows, lanes]))
                    charges.append(lax.select(what == 0, chg_in[2 * p + side, rows, lanes], held))
                red[h, p, out, :] = lax.select(mask, plane[0], plane[1])
                black[h, p, out, :] = lax.select(mask, plane[1], plane[0])
                source[RED, h, p, out, :] = lax.select(mask, charges[0], charges[1])
                source[BLACK, h, p, out, :] = lax.select(mask, charges[1], charges[0])

    def fresh_tiles(color, p, near, before, after, which):
        own, other = (red, black) if color == RED else (black, red)
        mask = parity_mask()
        lane = lax.broadcasted_iota(jnp.int32, (8, LANES), 1)
        first, second = (before, after) if color == RED else (after, before)
        factor = [[coef[n, h] for n in range(4)] for h in range(halves)]
        for tile in which:
            at = PAD + 8 * tile
            rows = pl.ds(at, 8)
            here = [other[h, near, rows, :] for h in range(halves)]
            outer, inner = beside(here, lane)
            result = []
            for h in range(halves):
                out_c, in_c, around_c, scale = factor[h]
                around = here[h] + lax.select(mask, other[h, first, rows, :], other[h, second, rows, :])
                along = other[h, near, pl.ds(at - 1, 8), :] + other[h, near, pl.ds(at + 1, 8), :]
                put = source[color, h, p, rows, :]
                old = own[h, p, rows, :]
                gathered = (put + along) + (out_c * outer[h] + in_c * inner[h]) + around_c * around
                fresh = scale * gathered - (RELAX - 1.0) * old
                result.append((lax.select(put < 0.5 * FIXED, fresh, old), here[h]))
            yield tile, result

    def update(color, p, near, before, after, which):
        own = red if color == RED else black
        for tile, result in fresh_tiles(color, p, near, before, after, which):
            for h, (value, _) in enumerate(result):
                own[h, p, pl.ds(PAD + 8 * tile, 8), :] = value

    def halo_black(exchange):
        return pairs + 2 * exchange, pairs + 2 * exchange + 1

    def outer_tiles(exchange):
        return tiles // 4 + 1 - exchange

    def spans(cut, piece):
        return [(0, cut), (tiles - cut, tiles)] if piece == 0 else [(cut, tiles - cut)]

    def jcopies(exchange, side, piece):
        moves = []
        for low, high in spans(outer_tiles(exchange), piece):
            plain = pl.ds(8 * low, 8 * (high - low))
            rows = pl.ds(PAD + 8 * low, 8 * (high - low))
            if exchange == PASSES:
                moves.append((full.at[(sectors, 1)[side], plain], full.at[(0, sectors + 1)[side], plain]))
                continue
            edge_pair = (pairs - 1, 0)[side]
            moves.append((black.at[:, edge_pair, rows], black.at[:, halo_black(exchange)[side], rows]))
            if exchange == 0:
                moves.append((mixed.at[side, :, plain], red.at[:, halo[side], rows]))
        return [
            pltpu.make_async_remote_copy(
                src_ref=src,
                dst_ref=dst,
                send_sem=jsend_sem.at[exchange, n, side, piece],
                recv_sem=jrecv_sem.at[exchange, n, side, piece],
                device_id={"phi": (right, left)[side]},
                device_id_type=MESH,
            )
            for n, (src, dst) in enumerate(moves)
        ]

    def on_j(exchange, piece, act):
        for side in range(2):
            for copy in jcopies(exchange, side, piece):
                act(copy)

    def mix(side):
        p = (pairs - 1, 0)[side]
        mask = parity_mask()
        for tile in range(tiles):
            rows = pl.ds(PAD + 8 * tile, 8)
            for h in range(halves):
                values, charges = red[h, p, rows, :], pltpu.roll(source[RED, h, p, rows, :], 1, axis=1)
                both = (charges, values) if side == 0 else (values, charges)
                mixed[side, h, pl.ds(8 * tile, 8), :] = lax.select(mask, *both)

    def unmix(piece):
        for low, high in spans(outer_tiles(0), piece):
            for tile in range(low, high):
                rows = pl.ds(PAD + 8 * tile, 8)
                for side in range(2):
                    for h in range(halves):
                        source[RED, h, halo[side], rows, :] = pltpu.roll(red[h, halo[side], rows, :], LANES - 1, axis=1)

    def zcopy(slot, side):
        return pltpu.make_async_remote_copy(
            src_ref=zsend.at[slot, side],
            dst_ref=zrecv.at[slot, side],
            send_sem=zsend_sem.at[slot, side],
            recv_sem=zrecv_sem.at[slot, side],
            device_id={"gz": (lax.rem(slab + 1, slabs), lax.rem(slab + slabs - 1, slabs))[side]},
            device_id_type=MESH,
        )

    def ccopy(exchange, side, face):
        return pltpu.make_async_remote_copy(
            src_ref=zsend.at[exchange, side, :, (pairs - 1, 0)[face]],
            dst_ref=crecv.at[exchange, side, face],
            send_sem=csend_sem.at[exchange, side, face],
            recv_sem=crecv_sem.at[exchange, side, face],
            device_id={
                "gz": (lax.rem(slab + 1, slabs), lax.rem(slab + slabs - 1, slabs))[side],
                "phi": (right, left)[face],
            },
            device_id_type=MESH,
        )

    def zmoves(exchange, side):
        rows = [zcopy(exchange, side)] + ([zcopy(PASSES, side)] if exchange == 0 else [])
        return [ccopy(exchange, side, face) for face in range(2)] + rows

    def on_z(exchange, act):
        for side in range(2):
            @pl.when((has_next, has_prev)[side])
            def _():
                for copy in zmoves(exchange, side):
                    act(copy)

    def send_z(exchange):
        def gather(p, _):
            for h in range(halves):
                zsend[exchange, 0, h, p] = black[h, p, pl.ds(PAD + depth - 2, 2), :]
                zsend[exchange, 1, h, p] = black[h, p, pl.ds(PAD, 2), :]
                if exchange == 0:
                    for side, at in ((0, PAD + depth - 1), (1, PAD)):
                        zsend[PASSES, side, h, p, pl.ds(0, 1), :] = red[h, p, pl.ds(at, 1), :]
                        zsend[PASSES, side, h, p, pl.ds(1, 1), :] = source[RED, h, p, pl.ds(at, 1), :]

        for p in range(pairs):
            gather(p, 0)

    def take_z(exchange):
        for side in range(2):
            @pl.when((has_prev, has_next)[side])
            def _():
                for copy in zmoves(exchange, side):
                    copy.wait_recv()
                two = pl.ds((PAD - 2, PAD + depth)[side], 2)
                one = pl.ds((PAD - 1, PAD + depth)[side], 1)
                for h in range(halves):
                    for p in range(pairs):
                        black[h, p, two, :] = zrecv[exchange, side, h, p]
                        if exchange == 0:
                            red[h, p, one, :] = zrecv[PASSES, side, h, p, pl.ds(0, 1), :]
                            source[RED, h, p, one, :] = zrecv[PASSES, side, h, p, pl.ds(1, 1), :]
                    for face in range(2):
                        black[h, halo_black(exchange)[face], two, :] = crecv[exchange, side, face, h]

    def loop(low, high, body, unroll=UNROLL):
        odd = (high - low) % unroll if unroll < high - low else high - low

        def several(n, _):
            for step in range(unroll):
                body(low + odd + n * unroll + step)
            return 0

        for p in range(low, low + odd):
            body(p)
        if odd < high - low:
            lax.fori_loop(0, (high - low) // unroll, several, 0)

    inside = range(1, tiles - 1)
    core = range(2, tiles - 2)
    rims = (0, tiles - 1)

    def red_inside(p):
        update(RED, p, p, p - 1, p + 1, inside)

    def finish(p, before, after, which, first):
        mask = parity_mask()
        sums = [[nothing if first else partial[h, 2 * p + side] for side in range(2)] for h in range(halves)]
        for tile, result in fresh_tiles(BLACK, p, p, before, after, which):
            for h, (value, near) in enumerate(result):
                for side in range(2):
                    plane = lax.select(mask, near, value) if side == 0 else lax.select(mask, value, near)
                    full[2 * p + 1 + side, pl.ds(8 * tile, 8), pl.ds(LANES * h, LANES)] = plane
                    sums[h][side] = sums[h][side] + plane
        for h in range(halves):
            for side in range(2):
                partial[h, 2 * p + side] = sums[h][side]

    def edges(sweep, piece):
        low, high = halo_black(sweep)
        on_j(sweep, piece, lambda copy: copy.wait_recv())
        if sweep == 0:
            unmix(piece)
        cut = outer_tiles(sweep)
        halo_tiles = [tile for low, high in spans(cut - 1, piece) for tile in range(low, high)]
        own_tiles = [tile for low, high in spans(cut, piece) for tile in range(low, high)]
        if piece == 0:
            own_tiles = [-1, *own_tiles, tiles]
        for side in range(2):
            p, before, after = ((0, low, 1), (pairs - 1, pairs - 2, high))[side]
            update(RED, p, p, before, after, own_tiles)
            p, near, before, after = ((halo[0], low, low, 0), (halo[1], high, pairs - 1, high))[side]
            update(RED, p, near, before, after, halo_tiles)
        for p, before, after in ((0, halo[0], 1), (pairs - 1, pairs - 2, halo[1])):
            if sweep < PASSES - 1:
                update(BLACK, p, p, before, after, halo_tiles)
            else:
                finish(p, before, after, halo_tiles, piece == 0)
        on_j(sweep + 1, piece, lambda copy: copy.start())

    for batch in ends:
        for copy in batch:
            copy.wait()
    loop(0, pairs, lambda p: prepare(p, rims))
    send_z(0)
    for p in (0, pairs - 1):
        for copy in pair_loads(p):
            copy.wait()
        prepare(p, inside)
    for side in range(2):
        mix(side)
    pl.semaphore_wait(barrier, 2 + 3 * (slabs - 1))
    on_z(0, lambda copy: copy.start())
    for piece in range(2):
        on_j(0, piece, lambda copy: copy.start())

    def arrive(p):
        for copy in pair_loads(p):
            copy.wait()
        prepare(p, inside)

    arrive(1)

    def arrive_and_update(p):
        arrive(p)
        red_inside(p - 1)

    loop(2, pairs - 1, arrive_and_update, 1)
    red_inside(pairs - 2)

    def black_rims(p):
        update(BLACK, p, p, p - 1, p + 1, rims)

    for sweep in range(PASSES):
        more = sweep < PASSES - 1
        take_z(sweep)
        loop(1, pairs - 1, lambda p: update(RED, p, p, p - 1, p + 1, (-1, 0, tiles - 1, tiles)), pairs - 2)
        if more:
            loop(2, pairs - 2, black_rims, pairs - 4)
        for piece in range(2):
            on_j(sweep, piece, lambda copy: copy.wait_send())
        edges(sweep, 0)
        if more:
            for p in (1, pairs - 2):
                black_rims(p)
            send_z(sweep + 1)
            on_z(sweep + 1, lambda copy: copy.start())
        edges(sweep, 1)
        if more:
            loop(1, pairs - 1, lambda p: update(BLACK, p, p, p - 1, p + 1, inside))
            on_z(sweep, lambda copy: copy.wait_send())
            loop(1, pairs - 1, red_inside)
        if sweep == PASSES - 2:
            loop(2, pairs - 2, lambda p: finish(p, p - 1, p + 1, core, True))

    for p in (1, pairs - 2):
        finish(p, p - 1, p + 1, range(tiles), True)
    loop(2, pairs - 2, lambda p: finish(p, p - 1, p + 1, (0, 1, tiles - 2, tiles - 1), False), pairs - 4)

    def add_up(group, _):
        for n in range(8):
            for h in range(halves):
                total[h, pl.ds(8 * group + n, 1), :] = jnp.sum(partial[h, 8 * group + n], axis=0, keepdims=True)
        return 0

    lax.fori_loop(0, sectors // 8, add_up, 0)
    for h in range(halves):
        edge[0, h] = total[h, pl.ds(sectors - 1, 1), :]
        edge[1, h] = total[h, pl.ds(0, 1), :]

    def tcopies(step):
        lower = lax.rem(slab + slabs - step, slabs)
        return [
            pltpu.make_async_remote_copy(
                src_ref=total,
                dst_ref=total_recv.at[step - 1],
                send_sem=tsend_sem.at[step - 1],
                recv_sem=trecv_sem.at[step - 1],
                device_id={"gz": lower},
                device_id_type=MESH,
            )
        ] + [
            pltpu.make_async_remote_copy(
                src_ref=edge.at[face],
                dst_ref=edge_recv.at[step - 1, face],
                send_sem=esend_sem.at[step - 1, face],
                recv_sem=erecv_sem.at[step - 1, face],
                device_id={"gz": lower, "phi": (right, left)[face]},
                device_id_type=MESH,
            )
            for face in range(2)
        ]

    for step in range(1, slabs):
        @pl.when(slab >= step)
        def _():
            for copy in tcopies(step):
                copy.start()

    carry[...] = jnp.zeros(carry.shape, jnp.float32)
    on_z(PASSES - 1, lambda copy: copy.wait_send())
    for step in range(1, slabs):
        @pl.when(slab + step < slabs)
        def _():
            for copy in tcopies(step):
                copy.wait_recv()
            for h in range(halves):
                carry[h, pl.ds(1, sectors), :] = carry[h, pl.ds(1, sectors), :] + total_recv[step - 1, h]
                for face, at in ((0, 0), (1, sectors + 1)):
                    carry[h, pl.ds(at, 1), :] = carry[h, pl.ds(at, 1), :] + edge_recv[step - 1, face, h]

    for piece in range(2):
        on_j(PASSES, piece, lambda copy: copy.wait())
    for step in range(1, slabs):
        @pl.when(slab >= step)
        def _():
            for copy in tcopies(step):
                copy.wait_send()


def drift_kernel(
    rings, full, carry, potential, shift_r, shift_phi,
    coef, runs, ones, twos, sums, out_r, out_phi, pot_sem, out_sem,
):
    halves = runs.shape[1]
    sectors = full.shape[0] - 2
    depth = full.shape[1]
    pairs = sectors // 2
    tiles = depth // 8
    row = lax.broadcasted_iota(jnp.int32, (8, LANES), 0)
    lane = lax.broadcasted_iota(jnp.int32, (8, LANES), 1)

    pot_copy = pltpu.make_async_copy(full.at[pl.ds(1, sectors)], potential, pot_sem)
    pot_copy.start()
    drift = 1.0 / (1.09 * 32.0)
    for h in range(halves):
        outward, inward, _, _, step = geometry(h, LANES * halves, sectors * rings)
        coef[0, h] = jnp.where(outward > 0.0, -0.5 * drift, 0.0)
        coef[1, h] = jnp.where(inward > 0.0, 0.5 * drift, 0.0)
        coef[2, h] = -0.5 * drift / step
        coef[3, h] = 0.3 * (-0.5 * drift / step)

    def out_copies(pair):
        planes = pl.ds(2 * pair, 2)
        return [
            pltpu.make_async_copy(src.at[planes], dst.at[planes], out_sem.at[n, pair])
            for n, (src, dst) in enumerate(((out_r, shift_r), (out_phi, shift_phi)))
        ]

    def integrate(plane, slot):
        for h in range(halves):
            after = jnp.broadcast_to(carry[h, pl.ds(plane, 1), :], (8, LANES))
            run = jnp.where(row == 0, after, 0.0)
            for ref in (runs, ones, twos):
                ref[slot, h, pl.ds(depth, 8), :] = run
            for tile in range(tiles - 1, -1, -1):
                run = run + full[plane, pl.ds(8 * tile, 8), pl.ds(LANES * h, LANES)]
                runs[slot, h, pl.ds(8 * tile, 8), :] = run
        for h in range(halves):
            for src, dst, hop in ((runs, ones, 1), (ones, twos, 2)):
                for tile in range(tiles - 1, -1, -1):
                    at = 8 * tile
                    dst[slot, h, pl.ds(at, 8), :] = src[slot, h, pl.ds(at, 8), :] + src[slot, h, pl.ds(at + hop, 8), :]
            for tile in range(tiles - 1, -1, -1):
                at = 8 * tile
                sums[plane, h, pl.ds(at, 8), :] = twos[slot, h, pl.ds(at, 8), :] + twos[slot, h, pl.ds(at + 4, 8), :]

    def combine(plane):
        for tile in range(tiles):
            rows = pl.ds(8 * tile, 8)
            outer, inner = beside([sums[plane, h, rows, :] for h in range(halves)], lane)
            for h in range(halves):
                lanes = pl.ds(LANES * h, LANES)
                along_r = coef[0, h] * outer[h] + coef[1, h] * inner[h]
                across = sums[plane + 1, h, rows, :] - sums[plane - 1, h, rows, :]
                out_r[plane - 1, rows, lanes] = along_r + coef[3, h] * across
                out_phi[plane - 1, rows, lanes] = coef[2, h] * across - 0.3 * along_r

    def emit(pair):
        combine(2 * pair + 1)
        combine(2 * pair + 2)
        for copy in out_copies(pair):
            copy.start()

    for plane in range(4):
        integrate(plane, plane % 2)

    def step(g, slot):
        integrate(2 * g, slot)
        integrate(2 * g + 1, slot + 1)
        emit(g - 2)

    group = STEPS if (pairs - 1) % STEPS == 0 else 1

    def body(n, _):
        for turn in range(group):
            step(2 + n * group + turn, 2 * (turn % 2))
        return 0

    lax.fori_loop(0, (pairs - 1) // group, body, 0)
    emit(pairs - 1)

    def drain(pair, _):
        for copy in out_copies(pair):
            copy.wait()
        return 0

    lax.fori_loop(0, pairs, drain, 0)
    pot_copy.wait()


def local(slabs, rings, potential_in, charge, cell_kind):
    sectors, depth, radial = potential_in.shape
    pairs, halves = sectors // 2, radial // LANES
    tall = depth + 2 * PAD
    any_spec = pl.BlockSpec(memory_space=pl.ANY)
    vmem_spec = pl.BlockSpec(memory_space=pltpu.VMEM)
    f32 = jnp.float32
    dma = pltpu.SemaphoreType.DMA
    full, carry = pl.pallas_call(
        functools.partial(relax_kernel, slabs, rings),
        out_shape=(
            pltpu.VMEM((sectors + 2, depth, radial), f32),
            pltpu.VMEM((halves, sectors + 2, LANES), f32),
        ),
        in_specs=[any_spec] * 3,
        out_specs=(vmem_spec, vmem_spec),
        scratch_shapes=[
            pltpu.VMEM((4, halves, 8, LANES), f32),
            pltpu.VMEM((sectors, depth, radial), f32),
            pltpu.VMEM((sectors, depth, radial), f32),
            pltpu.VMEM((sectors, depth, radial), jnp.int32),
            pltpu.VMEM((halves, pairs + 2, tall, LANES), f32),
            pltpu.VMEM((halves, pairs + 2 * PASSES, tall, LANES), f32),
            pltpu.VMEM((2, halves, pairs + 2, tall, LANES), f32),
            pltpu.VMEM((2, halves, depth, LANES), f32),
            pltpu.VMEM((PASSES + 1, 2, halves, pairs, 2, LANES), f32),
            pltpu.VMEM((PASSES + 1, 2, halves, pairs, 2, LANES), f32),
            pltpu.VMEM((PASSES, 2, 2, halves, 2, LANES), f32),
            pltpu.VMEM((halves, sectors, 8, LANES), f32),
            pltpu.VMEM((halves, sectors, LANES), f32),
            pltpu.VMEM((slabs - 1, halves, sectors, LANES), f32),
            pltpu.VMEM((2, halves, 1, LANES), f32),
            pltpu.VMEM((slabs - 1, 2, halves, 1, LANES), f32),
            dma((pairs + 2, 3)),
            dma((PASSES + 1, 4, 2, 2)),
            dma((PASSES + 1, 4, 2, 2)),
            dma((PASSES + 1, 2)),
            dma((PASSES + 1, 2)),
            dma((PASSES, 2, 2)),
            dma((PASSES, 2, 2)),
            dma((slabs - 1,)),
            dma((slabs - 1,)),
            dma((slabs - 1, 2)),
            dma((slabs - 1, 2)),
        ],
        compiler_params=pltpu.CompilerParams(
            collective_id=0, has_side_effects=True, vmem_limit_bytes=48 * 2**20
        ),
    )(potential_in, charge, cell_kind)

    full = pltpu.with_memory_space_constraint(full, pltpu.VMEM)
    carry = pltpu.with_memory_space_constraint(carry, pltpu.VMEM)
    block = jax.ShapeDtypeStruct((sectors, depth, radial), f32)
    return pl.pallas_call(
        functools.partial(drift_kernel, rings),
        out_shape=(block, block, block),
        in_specs=[vmem_spec, vmem_spec],
        out_specs=(any_spec,) * 3,
        scratch_shapes=[
            pltpu.VMEM((4, halves, 8, LANES), f32),
            pltpu.VMEM((4, halves, depth + 8, LANES), f32),
            pltpu.VMEM((4, halves, depth + 8, LANES), f32),
            pltpu.VMEM((4, halves, depth + 8, LANES), f32),
            pltpu.VMEM((sectors + 2, halves, depth, LANES), f32),
            pltpu.VMEM((sectors, depth, radial), f32),
            pltpu.VMEM((sectors, depth, radial), f32),
            dma,
            dma((2, pairs)),
        ],
        compiler_params=pltpu.CompilerParams(vmem_limit_bytes=24 * 2**20),
    )(full, carry)


def solution(mesh):
    spec = P("phi", "gz", None)
    body = functools.partial(local, mesh.shape["gz"], mesh.shape["phi"])
    return jax.shard_map(body, mesh=mesh, in_specs=(spec,) * 3, out_specs=(spec,) * 3, check_vma=False)
```

```python
import functools
import math

import jax
import jax.numpy as jnp
from jax import lax
from jax.experimental import pallas as pl
from jax.experimental.pallas import tpu as pltpu
from jax.sharding import PartitionSpec as P

PASSES = 3
RELAX = 1.5
FIXED = 1e30
MESH = pl.DeviceIdType.MESH
PAD = 16
LANES = 128
RED, BLACK = 0, 1
UNROLL = 2
STEPS = 3


def parity_mask():
    row = lax.broadcasted_iota(jnp.int32, (8, LANES), 0)
    lane = lax.broadcasted_iota(jnp.int32, (8, LANES), 1)
    return ((row + lane) & 1) == 0


def beside(halves, lane):
    ahead = [pltpu.roll(x, LANES - 1, axis=1) for x in halves]
    behind = [pltpu.roll(x, 1, axis=1) for x in halves]
    last = len(halves) - 1
    outer = [ahead[h] if h == last else lax.select(lane == LANES - 1, ahead[h + 1], ahead[h]) for h in range(last + 1)]
    inner = [behind[h] if h == 0 else lax.select(lane == 0, behind[h - 1], behind[h]) for h in range(last + 1)]
    return outer, inner


def geometry(half, radial, sectors):
    cell = lax.broadcasted_iota(jnp.int32, (8, LANES), 1) + LANES * half
    radius = radial * 0.5 + cell.astype(jnp.float32) + 0.5
    step = radius * (2.0 * math.pi / sectors)
    around = 1.0 / (step * step)
    outward = jnp.where(cell < radial - 1, 1.0 + 0.5 / radius, 0.0)
    inward = jnp.where(cell > 0, 1.0 - 0.5 / radius, 0.0)
    return outward, inward, around, 4.0 + 2.0 * around, step


def relax_kernel(
    slabs, rings, pot, chg, kind, full, carry,
    coef, pot_in, chg_in, kind_in, red, black, source, mixed, zsend, zrecv, crecv,
    partial, total, total_recv, edge, edge_recv,
    load_sem, jsend_sem, jrecv_sem, zsend_sem, zrecv_sem, csend_sem, crecv_sem,
    tsend_sem, trecv_sem, esend_sem, erecv_sem,
):
    halves = red.shape[0]
    sectors, depth, radial = pot_in.shape
    pairs = sectors // 2
    tiles = depth // 8
    slab = lax.axis_index("gz")
    ring = lax.axis_index("phi")
    right, left = lax.rem(ring + 1, rings), lax.rem(ring + rings - 1, rings)
    has_next, has_prev = slab < slabs - 1, slab > 0
    halo = (pairs, pairs + 1)

    def loads(slot, planes, rows):
        return [
            pltpu.make_async_copy(src.at[planes, rows], dst.at[planes, rows], load_sem.at[slot, n])
            for n, (src, dst) in enumerate(((pot, pot_in), (chg, chg_in), (kind, kind_in)))
        ]

    every, middle = pl.ds(0, sectors), pl.ds(8, depth - 16)
    ends = [loads(pairs, every, pl.ds(0, 8)), loads(pairs + 1, every, pl.ds(depth - 8, 8))]

    def pair_loads(p):
        return loads(p, pl.ds(2 * p, 2), middle)

    for batch in ends:
        for copy in batch:
            copy.start()
    for p in (0, pairs - 1):
        for copy in pair_loads(p):
            copy.start()

    def start_pair(p, _):
        for copy in pair_loads(p):
            copy.start()
        return 0

    lax.fori_loop(1, pairs - 1, start_pair, 0)

    barrier = pltpu.get_barrier_semaphore()
    for neighbour in (left, right):
        pl.semaphore_signal(barrier, inc=1, device_id={"phi": neighbour}, device_id_type=MESH)
    for step in range(1, slabs):
        peer = lax.rem(slab + step, slabs)
        for column in (left, ring, right):
            pl.semaphore_signal(barrier, inc=1, device_id={"gz": peer, "phi": column}, device_id_type=MESH)

    for h in range(halves):
        outward, inward, around_i, diag, _ = geometry(h, radial, sectors * rings)
        for n, values in enumerate((outward, inward, around_i, RELAX / diag)):
            coef[n, h] = values

    nothing = jnp.zeros((8, LANES), jnp.float32)
    held = jnp.full((8, LANES), FIXED, jnp.float32)

    def clear(p, _):
        for h in range(halves):
            for rows in (pl.ds(PAD - 8, 8), pl.ds(PAD + depth, 8)):
                black[h, p, rows, :] = nothing
        return 0

    def clear_own(p, _):
        for h in range(halves):
            for rows in (pl.ds(PAD - 8, 8), pl.ds(PAD + depth, 8)):
                red[h, p, rows, :] = nothing
                source[RED, h, p, rows, :] = held
        return 0

    lax.fori_loop(0, black.shape[1], clear, 0)
    lax.fori_loop(0, pairs, clear_own, 0)

    def prepare(p, which):
        mask = parity_mask()
        for tile in which:
            rows, out = pl.ds(8 * tile, 8), pl.ds(PAD + 8 * tile, 8)
            for h in range(halves):
                lanes = pl.ds(LANES * h, LANES)
                plane, charges = [], []
                for side in range(2):
                    what = kind_in[2 * p + side, rows, lanes]
                    plane.append(lax.select(what == 1, nothing, pot_in[2 * p + side, rows, lanes]))
                    charges.append(lax.select(what == 0, chg_in[2 * p + side, rows, lanes], held))
                red[h, p, out, :] = lax.select(mask, plane[0], plane[1])
                black[h, p, out, :] = lax.select(mask, plane[1], plane[0])
                source[RED, h, p, out, :] = lax.select(mask, charges[0], charges[1])
                source[BLACK, h, p, out, :] = lax.select(mask, charges[1], charges[0])

    def fresh_tiles(color, p, near, before, after, which):
        own, other = (red, black) if color == RED else (black, red)
        mask = parity_mask()
        lane = lax.broadcasted_iota(jnp.int32, (8, LANES), 1)
        first, second = (before, after) if color == RED else (after, before)
        factor = [[coef[n, h] for n in range(4)] for h in range(halves)]
        for tile in which:
            at = PAD + 8 * tile
            rows = pl.ds(at, 8)
            here = [other[h, near, rows, :] for h in range(halves)]
            outer, inner = beside(here, lane)
            result = []
            for h in range(halves):
                out_c, in_c, around_c, scale = factor[h]
                around = here[h] + lax.select(mask, other[h, first, rows, :], other[h, second, rows, :])
                along = other[h, near, pl.ds(at - 1, 8), :] + other[h, near, pl.ds(at + 1, 8), :]
                put = source[color, h, p, rows, :]
                old = own[h, p, rows, :]
                gathered = (put + along) + (out_c * outer[h] + in_c * inner[h]) + around_c * around
                fresh = scale * gathered - (RELAX - 1.0) * old
                result.append((lax.select(put < 0.5 * FIXED, fresh, old), here[h]))
            yield tile, result

    def update(color, p, near, before, after, which):
        own = red if color == RED else black
        for tile, result in fresh_tiles(color, p, near, before, after, which):
            for h, (value, _) in enumerate(result):
                own[h, p, pl.ds(PAD + 8 * tile, 8), :] = value

    def halo_black(exchange):
        return pairs + 2 * exchange, pairs + 2 * exchange + 1

    def outer_tiles(exchange):
        return tiles // 4 - exchange

    def spans(cut, piece):
        return [(0, cut), (tiles - cut, tiles)] if piece == 0 else [(cut, tiles - cut)]

    def jcopies(exchange, side, piece):
        moves = []
        for low, high in spans(outer_tiles(exchange), piece):
            plain = pl.ds(8 * low, 8 * (high - low))
            rows = pl.ds(PAD + 8 * low, 8 * (high - low))
            if exchange == PASSES:
                moves.append((full.at[(sectors, 1)[side], plain], full.at[(0, sectors + 1)[side], plain]))
                continue
            edge_pair = (pairs - 1, 0)[side]
            moves.append((black.at[:, edge_pair, rows], black.at[:, halo_black(exchange)[side], rows]))
            if exchange == 0:
                moves.append((mixed.at[side, :, plain], red.at[:, halo[side], rows]))
        return [
            pltpu.make_async_remote_copy(
                src_ref=src,
                dst_ref=dst,
                send_sem=jsend_sem.at[exchange, n, side, piece],
                recv_sem=jrecv_sem.at[exchange, n, side, piece],
                device_id={"phi": (right, left)[side]},
                device_id_type=MESH,
            )
            for n, (src, dst) in enumerate(moves)
        ]

    def on_j(exchange, piece, act):
        for side in range(2):
            for copy in jcopies(exchange, side, piece):
                act(copy)

    def mix(side):
        p = (pairs - 1, 0)[side]
        mask = parity_mask()
        for tile in range(tiles):
            rows = pl.ds(PAD + 8 * tile, 8)
            for h in range(halves):
                values, charges = red[h, p, rows, :], pltpu.roll(source[RED, h, p, rows, :], 1, axis=1)
                both = (charges, values) if side == 0 else (values, charges)
                mixed[side, h, pl.ds(8 * tile, 8), :] = lax.select(mask, *both)

    def unmix(piece):
        for low, high in spans(outer_tiles(0), piece):
            for tile in range(low, high):
                rows = pl.ds(PAD + 8 * tile, 8)
                for side in range(2):
                    for h in range(halves):
                        source[RED, h, halo[side], rows, :] = pltpu.roll(red[h, halo[side], rows, :], LANES - 1, axis=1)

    def zcopy(slot, side):
        return pltpu.make_async_remote_copy(
            src_ref=zsend.at[slot, side],
            dst_ref=zrecv.at[slot, side],
            send_sem=zsend_sem.at[slot, side],
            recv_sem=zrecv_sem.at[slot, side],
            device_id={"gz": (lax.rem(slab + 1, slabs), lax.rem(slab + slabs - 1, slabs))[side]},
            device_id_type=MESH,
        )

    def ccopy(exchange, side, face):
        return pltpu.make_async_remote_copy(
            src_ref=zsend.at[exchange, side, :, (pairs - 1, 0)[face]],
            dst_ref=crecv.at[exchange, side, face],
            send_sem=csend_sem.at[exchange, side, face],
            recv_sem=crecv_sem.at[exchange, side, face],
            device_id={
                "gz": (lax.rem(slab + 1, slabs), lax.rem(slab + slabs - 1, slabs))[side],
                "phi": (right, left)[face],
            },
            device_id_type=MESH,
        )

    def zmoves(exchange, side):
        rows = [zcopy(exchange, side)] + ([zcopy(PASSES, side)] if exchange == 0 else [])
        return [ccopy(exchange, side, face) for face in range(2)] + rows

    def on_z(exchange, act):
        for side in range(2):
            @pl.when((has_next, has_prev)[side])
            def _():
                for copy in zmoves(exchange, side):
                    act(copy)

    def send_z(exchange):
        def gather(p, _):
            for h in range(halves):
                zsend[exchange, 0, h, p] = black[h, p, pl.ds(PAD + depth - 2, 2), :]
                zsend[exchange, 1, h, p] = black[h, p, pl.ds(PAD, 2), :]
                if exchange == 0:
                    for side, at in ((0, PAD + depth - 1), (1, PAD)):
                        zsend[PASSES, side, h, p, pl.ds(0, 1), :] = red[h, p, pl.ds(at, 1), :]
                        zsend[PASSES, side, h, p, pl.ds(1, 1), :] = source[RED, h, p, pl.ds(at, 1), :]

        for p in range(pairs):
            gather(p, 0)

    def take_z(exchange):
        for side in range(2):
            @pl.when((has_prev, has_next)[side])
            def _():
                for copy in zmoves(exchange, side):
                    copy.wait_recv()
                two = pl.ds((PAD - 2, PAD + depth)[side], 2)
                one = pl.ds((PAD - 1, PAD + depth)[side], 1)
                for h in range(halves):
                    for p in range(pairs):
                        black[h, p, two, :] = zrecv[exchange, side, h, p]
                        if exchange == 0:
                            red[h, p, one, :] = zrecv[PASSES, side, h, p, pl.ds(0, 1), :]
                            source[RED, h, p, one, :] = zrecv[PASSES, side, h, p, pl.ds(1, 1), :]
                    for face in range(2):
                        black[h, halo_black(exchange)[face], two, :] = crecv[exchange, side, face, h]

    def loop(low, high, body, unroll=UNROLL):
        odd = (high - low) % unroll if unroll < high - low else high - low

        def several(n, _):
            for step in range(unroll):
                body(low + odd + n * unroll + step)
            return 0

        for p in range(low, low + odd):
            body(p)
        if odd < high - low:
            lax.fori_loop(0, (high - low) // unroll, several, 0)

    inside = range(1, tiles - 1)
    core = range(2, tiles - 2)
    rims = (0, tiles - 1)

    def red_inside(p):
        update(RED, p, p, p - 1, p + 1, inside)

    def finish(p, before, after, which, first):
        mask = parity_mask()
        sums = [[nothing if first else partial[h, 2 * p + side] for side in range(2)] for h in range(halves)]
        for tile, result in fresh_tiles(BLACK, p, p, before, after, which):
            for h, (value, near) in enumerate(result):
                for side in range(2):
                    plane = lax.select(mask, near, value) if side == 0 else lax.select(mask, value, near)
                    full[2 * p + 1 + side, pl.ds(8 * tile, 8), pl.ds(LANES * h, LANES)] = plane
                    sums[h][side] = sums[h][side] + plane
        for h in range(halves):
            for side in range(2):
                partial[h, 2 * p + side] = sums[h][side]

    def edges(sweep, piece):
        low, high = halo_black(sweep)
        on_j(sweep, piece, lambda copy: copy.wait_recv())
        if sweep == 0:
            unmix(piece)
        cut = outer_tiles(sweep)
        halo_tiles = [tile for low, high in spans(cut - 1, piece) for tile in range(low, high)]
        own_tiles = [tile for low, high in spans(cut, piece) for tile in range(low, high)]
        if piece == 0:
            own_tiles = [-1, *own_tiles, tiles]
        for side in range(2):
            p, before, after = ((0, low, 1), (pairs - 1, pairs - 2, high))[side]
            update(RED, p, p, before, after, own_tiles)
            p, near, before, after = ((halo[0], low, low, 0), (halo[1], high, pairs - 1, high))[side]
            update(RED, p, near, before, after, halo_tiles)
        for p, before, after in ((0, halo[0], 1), (pairs - 1, pairs - 2, halo[1])):
            if sweep < PASSES - 1:
                update(BLACK, p, p, before, after, halo_tiles)
            else:
                finish(p, before, after, halo_tiles, piece == 0)
        on_j(sweep + 1, piece, lambda copy: copy.start())

    for batch in ends:
        for copy in batch:
            copy.wait()
    loop(0, pairs, lambda p: prepare(p, rims))
    send_z(0)
    for p in (0, pairs - 1):
        for copy in pair_loads(p):
            copy.wait()
        prepare(p, inside)
    for side in range(2):
        mix(side)
    pl.semaphore_wait(barrier, 2 + 3 * (slabs - 1))
    for piece in range(2):
        on_j(0, piece, lambda copy: copy.start())
    on_z(0, lambda copy: copy.start())

    def arrive(p):
        for copy in pair_loads(p):
            copy.wait()
        prepare(p, inside)

    arrive(1)

    def arrive_and_update(p):
        arrive(p)
        red_inside(p - 1)

    loop(2, pairs - 1, arrive_and_update, 1)
    red_inside(pairs - 2)

    def black_rims(p):
        update(BLACK, p, p, p - 1, p + 1, rims)

    for sweep in range(PASSES):
        more = sweep < PASSES - 1
        take_z(sweep)
        loop(1, pairs - 1, lambda p: update(RED, p, p, p - 1, p + 1, (-1, 0, tiles - 1, tiles)), pairs - 2)
        if more:
            loop(2, pairs - 2, black_rims, pairs - 4)
        for piece in range(2):
            on_j(sweep, piece, lambda copy: copy.wait_send())
        edges(sweep, 0)
        if more:
            for p in (1, pairs - 2):
                black_rims(p)
            send_z(sweep + 1)
            on_z(sweep + 1, lambda copy: copy.start())
        edges(sweep, 1)
        if more:
            loop(1, pairs - 1, lambda p: update(BLACK, p, p, p - 1, p + 1, inside))
            on_z(sweep, lambda copy: copy.wait_send())
            loop(1, pairs - 1, red_inside)
        if sweep == PASSES - 2:
            loop(2, pairs - 2, lambda p: finish(p, p - 1, p + 1, core, True))

    for p in (1, pairs - 2):
        finish(p, p - 1, p + 1, range(tiles), True)
    loop(2, pairs - 2, lambda p: finish(p, p - 1, p + 1, (0, 1, tiles - 2, tiles - 1), False), pairs - 4)

    def add_up(group, _):
        for n in range(8):
            for h in range(halves):
                total[h, pl.ds(8 * group + n, 1), :] = jnp.sum(partial[h, 8 * group + n], axis=0, keepdims=True)
        return 0

    lax.fori_loop(0, sectors // 8, add_up, 0)
    for h in range(halves):
        edge[0, h] = total[h, pl.ds(sectors - 1, 1), :]
        edge[1, h] = total[h, pl.ds(0, 1), :]

    def tcopies(step):
        lower = lax.rem(slab + slabs - step, slabs)
        return [
            pltpu.make_async_remote_copy(
                src_ref=total,
                dst_ref=total_recv.at[step - 1],
                send_sem=tsend_sem.at[step - 1],
                recv_sem=trecv_sem.at[step - 1],
                device_id={"gz": lower},
                device_id_type=MESH,
            )
        ] + [
            pltpu.make_async_remote_copy(
                src_ref=edge.at[face],
                dst_ref=edge_recv.at[step - 1, face],
                send_sem=esend_sem.at[step - 1, face],
                recv_sem=erecv_sem.at[step - 1, face],
                device_id={"gz": lower, "phi": (right, left)[face]},
                device_id_type=MESH,
            )
            for face in range(2)
        ]

    for step in range(1, slabs):
        @pl.when(slab >= step)
        def _():
            for copy in tcopies(step):
                copy.start()

    carry[...] = jnp.zeros(carry.shape, jnp.float32)
    on_z(PASSES - 1, lambda copy: copy.wait_send())
    for step in range(1, slabs):
        @pl.when(slab + step < slabs)
        def _():
            for copy in tcopies(step):
                copy.wait_recv()
            for h in range(halves):
                carry[h, pl.ds(1, sectors), :] = carry[h, pl.ds(1, sectors), :] + total_recv[step - 1, h]
                for face, at in ((0, 0), (1, sectors + 1)):
                    carry[h, pl.ds(at, 1), :] = carry[h, pl.ds(at, 1), :] + edge_recv[step - 1, face, h]

    for piece in range(2):
        on_j(PASSES, piece, lambda copy: copy.wait())
    for step in range(1, slabs):
        @pl.when(slab >= step)
        def _():
            for copy in tcopies(step):
                copy.wait_send()


def drift_kernel(
    rings, full, carry, potential, shift_r, shift_phi,
    coef, runs, ones, twos, sums, out_r, out_phi, pot_sem, out_sem,
):
    halves = runs.shape[1]
    sectors = full.shape[0] - 2
    depth = full.shape[1]
    pairs = sectors // 2
    tiles = depth // 8
    row = lax.broadcasted_iota(jnp.int32, (8, LANES), 0)
    lane = lax.broadcasted_iota(jnp.int32, (8, LANES), 1)

    pot_copy = pltpu.make_async_copy(full.at[pl.ds(1, sectors)], potential, pot_sem)
    pot_copy.start()
    drift = 1.0 / (1.09 * 32.0)
    for h in range(halves):
        outward, inward, _, _, step = geometry(h, LANES * halves, sectors * rings)
        coef[0, h] = jnp.where(outward > 0.0, -0.5 * drift, 0.0)
        coef[1, h] = jnp.where(inward > 0.0, 0.5 * drift, 0.0)
        coef[2, h] = -0.5 * drift / step
        coef[3, h] = 0.3 * (-0.5 * drift / step)

    def out_copies(pair):
        planes = pl.ds(2 * pair, 2)
        return [
            pltpu.make_async_copy(src.at[planes], dst.at[planes], out_sem.at[n, pair])
            for n, (src, dst) in enumerate(((out_r, shift_r), (out_phi, shift_phi)))
        ]

    def integrate(plane, slot):
        for h in range(halves):
            after = jnp.broadcast_to(carry[h, pl.ds(plane, 1), :], (8, LANES))
            run = jnp.where(row == 0, after, 0.0)
            for ref in (runs, ones, twos):
                ref[slot, h, pl.ds(depth, 8), :] = run
            for tile in range(tiles - 1, -1, -1):
                run = run + full[plane, pl.ds(8 * tile, 8), pl.ds(LANES * h, LANES)]
                runs[slot, h, pl.ds(8 * tile, 8), :] = run
        for h in range(halves):
            for src, dst, hop in ((runs, ones, 1), (ones, twos, 2)):
                for tile in range(tiles - 1, -1, -1):
                    at = 8 * tile
                    dst[slot, h, pl.ds(at, 8), :] = src[slot, h, pl.ds(at, 8), :] + src[slot, h, pl.ds(at + hop, 8), :]
            for tile in range(tiles - 1, -1, -1):
                at = 8 * tile
                sums[plane, h, pl.ds(at, 8), :] = twos[slot, h, pl.ds(at, 8), :] + twos[slot, h, pl.ds(at + 4, 8), :]

    def combine(plane):
        for tile in range(tiles):
            rows = pl.ds(8 * tile, 8)
            outer, inner = beside([sums[plane, h, rows, :] for h in range(halves)], lane)
            for h in range(halves):
                lanes = pl.ds(LANES * h, LANES)
                along_r = coef[0, h] * outer[h] + coef[1, h] * inner[h]
                across = sums[plane + 1, h, rows, :] - sums[plane - 1, h, rows, :]
                out_r[plane - 1, rows, lanes] = along_r + coef[3, h] * across
                out_phi[plane - 1, rows, lanes] = coef[2, h] * across - 0.3 * along_r

    def emit(pair):
        combine(2 * pair + 1)
        combine(2 * pair + 2)
        for copy in out_copies(pair):
            copy.start()

    for plane in range(4):
        integrate(plane, plane % 2)

    def step(g, slot):
        integrate(2 * g, slot)
        integrate(2 * g + 1, slot + 1)
        emit(g - 2)

    group = STEPS if (pairs - 1) % STEPS == 0 else 1

    def body(n, _):
        for turn in range(group):
            step(2 + n * group + turn, 2 * (turn % 2))
        return 0

    lax.fori_loop(0, (pairs - 1) // group, body, 0)
    emit(pairs - 1)

    def drain(pair, _):
        for copy in out_copies(pair):
            copy.wait()
        return 0

    lax.fori_loop(0, pairs, drain, 0)
    pot_copy.wait()


def local(slabs, rings, potential_in, charge, cell_kind):
    sectors, depth, radial = potential_in.shape
    pairs, halves = sectors // 2, radial // LANES
    tall = depth + 2 * PAD
    any_spec = pl.BlockSpec(memory_space=pl.ANY)
    vmem_spec = pl.BlockSpec(memory_space=pltpu.VMEM)
    f32 = jnp.float32
    dma = pltpu.SemaphoreType.DMA
    full, carry = pl.pallas_call(
        functools.partial(relax_kernel, slabs, rings),
        out_shape=(
            pltpu.VMEM((sectors + 2, depth, radial), f32),
            pltpu.VMEM((halves, sectors + 2, LANES), f32),
        ),
        in_specs=[any_spec] * 3,
        out_specs=(vmem_spec, vmem_spec),
        scratch_shapes=[
            pltpu.VMEM((4, halves, 8, LANES), f32),
            pltpu.VMEM((sectors, depth, radial), f32),
            pltpu.VMEM((sectors, depth, radial), f32),
            pltpu.VMEM((sectors, depth, radial), jnp.int32),
            pltpu.VMEM((halves, pairs + 2, tall, LANES), f32),
            pltpu.VMEM((halves, pairs + 2 * PASSES, tall, LANES), f32),
            pltpu.VMEM((2, halves, pairs + 2, tall, LANES), f32),
            pltpu.VMEM((2, halves, depth, LANES), f32),
            pltpu.VMEM((PASSES + 1, 2, halves, pairs, 2, LANES), f32),
            pltpu.VMEM((PASSES + 1, 2, halves, pairs, 2, LANES), f32),
            pltpu.VMEM((PASSES, 2, 2, halves, 2, LANES), f32),
            pltpu.VMEM((halves, sectors, 8, LANES), f32),
            pltpu.VMEM((halves, sectors, LANES), f32),
            pltpu.VMEM((slabs - 1, halves, sectors, LANES), f32),
            pltpu.VMEM((2, halves, 1, LANES), f32),
            pltpu.VMEM((slabs - 1, 2, halves, 1, LANES), f32),
            dma((pairs + 2, 3)),
            dma((PASSES + 1, 4, 2, 2)),
            dma((PASSES + 1, 4, 2, 2)),
            dma((PASSES + 1, 2)),
            dma((PASSES + 1, 2)),
            dma((PASSES, 2, 2)),
            dma((PASSES, 2, 2)),
            dma((slabs - 1,)),
            dma((slabs - 1,)),
            dma((slabs - 1, 2)),
            dma((slabs - 1, 2)),
        ],
        compiler_params=pltpu.CompilerParams(
            collective_id=0, has_side_effects=True, vmem_limit_bytes=48 * 2**20
        ),
    )(potential_in, charge, cell_kind)

    full = pltpu.with_memory_space_constraint(full, pltpu.VMEM)
    carry = pltpu.with_memory_space_constraint(carry, pltpu.VMEM)
    block = jax.ShapeDtypeStruct((sectors, depth, radial), f32)
    return pl.pallas_call(
        functools.partial(drift_kernel, rings),
        out_shape=(block, block, block),
        in_specs=[vmem_spec, vmem_spec],
        out_specs=(any_spec,) * 3,
        scratch_shapes=[
            pltpu.VMEM((4, halves, 8, LANES), f32),
            pltpu.VMEM((4, halves, depth + 8, LANES), f32),
            pltpu.VMEM((4, halves, depth + 8, LANES), f32),
            pltpu.VMEM((4, halves, depth + 8, LANES), f32),
            pltpu.VMEM((sectors + 2, halves, depth, LANES), f32),
            pltpu.VMEM((sectors, depth, radial), f32),
            pltpu.VMEM((sectors, depth, radial), f32),
            dma,
            dma((2, pairs)),
        ],
        compiler_params=pltpu.CompilerParams(vmem_limit_bytes=24 * 2**20),
    )(full, carry)


def solution(mesh):
    spec = P("phi", "gz", None)
    body = functools.partial(local, mesh.shape["gz"], mesh.shape["phi"])
    return jax.shard_map(body, mesh=mesh, in_specs=(spec,) * 3, out_specs=(spec,) * 3, check_vma=False)
```
